512 devices in a mesh: gx: 32 (over x, z_hi, core), yz: 16 (over z_lo, y).
Axes of the slice: x: 4, y: 4, z: 16 (z_hi: 4, z_lo: 4; z = z_hi * 4 + z_lo), core: 2. Of those that a mesh axis runs over, the one named last changes fastest.
Arguments:
- velocity: float32 [3, 64, 128, 128], P(None, 'gx', 'yz'), may hold values from -6 to 6
- viscosity: float32 [64, 128, 128], P('gx', 'yz'), may hold values from 0.1 to 1
- cotangent: float32 [3, 64, 128, 128], P(None, 'gx', 'yz'), may hold values from -6 to 6
- assignment: int32 [8192, 1], P(('gx', 'yz')), may hold values from 0 to 15; in each aligned block of 16 rows (0 to 15, 16 to 31, ...) at most 2 rows name the same one
- w_in: float32 [16, 9, 128], P('yz'), may hold values from -2 to 2
- b_in: float32 [16, 128], P('yz'), may hold values from -3 to 3
- w_mid: float32 [16, 128, 128], P('yz'), may hold values from -0.5 to 0.5
- b_mid: float32 [16, 128], P('yz'), may hold values from -3 to 3
- w_out: float32 [16, 128, 6], P('yz'), may hold values from -0.5 to 0.5
- b_out: float32 [16, 6], P('yz'), may hold values from -3 to 3
Outputs:
- predicted: float32 [3, 64, 128, 128], P(None, 'gx', 'yz')
- grad_velocity: float32 [3, 64, 128, 128], P(None, 'gx', 'yz')
- grad_w_in: float32 [16, 9, 128], P('yz')
- grad_b_in: float32 [16, 128], P('yz')
- grad_w_mid: float32 [16, 128, 128], P('yz')
- grad_b_mid: float32 [16, 128], P('yz')
- grad_w_out: float32 [16, 128, 6], P('yz')
- grad_b_out: float32 [16, 6], P('yz')
The draws below stay inside these ranges and needn't reach their ends.
Inputs may be any that keep to these rules, and one draw needn't show every extreme that they name: `assignment`: of the 16 rows of one device, at most 2 name any one network.
All inputs are finite; a program needn't handle non-finite values.
Results may differ from the reference program's by a relative error of at most 0.00019.
Values sent between devices are 32-bit elements; how exact they have to be, the bound alone decides.
No kernel may reach another device: no remote copies, remote signals or barrier semaphores. Data moves between devices by JAX's collectives and lax.ppermute only.
A program may use at most 64 MiB of HBM per device.

```python
import math
import jax
import jax.numpy as jnp
import numpy as np
from jax import lax

CX = 2
CY = 8
NZ = 128
HIDDEN_SIZE = 128
SUBSTEPS = 4
EXPERTS = 16
CAP = 2
NX = 64
NY = 128
COLUMNS = 8192
N_GX = 32
N_YZ = 16


def block_levels(rng, extent, cuts, low, largest):
    def one(position, blocks):
        draws = jax.random.uniform(jax.random.fold_in(jax.random.fold_in(rng, 6), position), (blocks,), jnp.float32, low / len(cuts), largest / len(cuts))
        return jnp.repeat(jnp.exp(draws), extent[position] // blocks).reshape((-1,) + (1,) * (len(extent) - position - 1))

    level = one(*cuts[0])
    for cut in cuts[1:]:
        level = level * one(*cut)
    return level


def shared_out(rng, own, number, rows, number_of, top, limit, lean):
    sequence = jax.random.permutation(rng, number_of)
    crowded, ordinary = load_shares(number_of, rows * top, limit, lean, True), load_shares(number_of, rows * top, limit, lean, False)
    places = jnp.arange(number_of)

    def named(sizes, rotation):
        used = int((sizes > 0).sum())
        fixed = max(1, used // 4)
        passed = fixed + (places - fixed + rotation * (used - fixed)) % max(1, number_of - fixed)
        return jnp.zeros((number_of,), jnp.int32).at[sequence[jnp.where(places < fixed, places, passed)]].set(jnp.asarray(sizes, jnp.int32))

    sizes = jnp.where(number % 4 == 0, named(crowded, number // 4), named(ordinary, number - number // 4 - 1))
    mixed = jax.random.permutation(jax.random.fold_in(own, 3), number_of)
    source_of, receiver = mixed[0:number_of // 2 * 2:2], mixed[1:number_of // 2 * 2:2]
    margin = jnp.minimum(sizes[source_of] - 1, limit - sizes[receiver]) // 2
    margin = jnp.where((source_of == sequence[0]) | (receiver == sequence[0]) | (sizes[receiver] == 0), 0, jnp.maximum(margin, 0))
    passed = jax.random.randint(jax.random.fold_in(own, 4), (number_of // 2,), 0, 1 << 20) % (margin + 1)
    sizes = sizes.at[source_of].add(-passed).at[receiver].add(passed)
    labels = jnp.searchsorted(jnp.cumsum(sizes), jnp.arange(rows * top), side="right").astype(jnp.int32)
    table = labels.reshape(top, rows).T
    table = table[jax.random.permutation(jax.random.fold_in(own, 1), rows)]
    rotation = jax.random.randint(jax.random.fold_in(own, 2), (rows, 1), 0, top)
    return jnp.take_along_axis(table, (jnp.arange(top)[None, :] + rotation) % top, axis=1)


def load_shares(number_of, total, most, skew, full):
    portions = [(1 << 20) // math.isqrt(grade ** skew) + 1 for grade in range(1, number_of + 1)]
    largest = most if full else min(most, max(-(-total // number_of), total * portions[0] // sum(portions)))
    least = 1 if total - largest >= number_of - 1 else 0
    given, surplus = [largest] + [least] * (number_of - 1), total - largest - least * (number_of - 1)
    while surplus > 0:
        candidates = [i for i in range(1, number_of) if given[i] < largest] or [i for i in range(1, number_of) if given[i] < most]
        mass, left = sum([portions[i] for i in candidates]), surplus
        for i in candidates:
            more = min(most - given[i], max(1, left * portions[i] // mass), surplus)
            given[i] = given[i] + more
            surplus = surplus - more
    return np.array(given)


def gaussian(own_key, shape, spread, limit, shards=(), kind=jnp.bfloat16):
    factor_of = block_levels(own_key, shape, shards, -0.22, 0.18) if shards else 1.0
    drawn = jax.random.normal(own_key, shape, jnp.float32) * spread * factor_of
    return jnp.minimum(jnp.maximum(drawn, -limit), limit).astype(kind)


def setup_inputs(seed: int = 0) -> dict:
    key_of = jax.random.split(jax.random.key(seed), 11)
    velocity = gaussian(key_of[0], (3, NX, NY, NZ), 1.0, 6.0, ((1, 32), (2, 16)), jnp.float32)
    viscosity = jnp.clip(jnp.exp(math.log(1.0) - 2.3025851 * jax.random.uniform(key_of[1], (NX, NY, NZ), jnp.float32) ** block_levels(key_of[1], (NX, NY, NZ), ((0, 32), (1, 16)), -0.2, 0.2)), 0.1, 1.0)
    cotangent = gaussian(key_of[2], (3, NX, NY, NZ), 1.0, 6.0, ((1, 32), (2, 16)), jnp.float32)
    assignment_keys = jax.random.split(jax.random.fold_in(key_of[3], 1), COLUMNS // (CX * CY))
    assignment_turns = jax.random.permutation(jax.random.fold_in(key_of[3], 3), COLUMNS // (CX * CY))
    assignment = jax.vmap(lambda own, number: shared_out(jax.random.fold_in(key_of[3], 2), own, number, CX * CY, EXPERTS, 1, CAP, 2))(assignment_keys, assignment_turns).reshape((COLUMNS, 1))
    w_in = gaussian(key_of[4], (EXPERTS, 9, HIDDEN_SIZE), 9 ** -0.5, 2.0, ((0, 16),), jnp.float32)
    b_in = gaussian(key_of[5], (EXPERTS, HIDDEN_SIZE), 0.5, 3.0, ((0, 16),), jnp.float32)
    w_mid = gaussian(key_of[6], (EXPERTS, HIDDEN_SIZE, HIDDEN_SIZE), HIDDEN_SIZE ** -0.5, 0.5, ((0, 16),), jnp.float32)
    b_mid = gaussian(key_of[7], (EXPERTS, HIDDEN_SIZE), 0.5, 3.0, ((0, 16),), jnp.float32)
    w_out = gaussian(key_of[8], (EXPERTS, HIDDEN_SIZE, 6), HIDDEN_SIZE ** -0.5, 0.5, ((0, 16),), jnp.float32)
    b_out = gaussian(key_of[9], (EXPERTS, 6), 0.5, 3.0, ((0, 16),), jnp.float32)
    return {"velocity": velocity, "viscosity": viscosity, "cotangent": cotangent, "assignment": assignment, "w_in": w_in, "b_in": b_in, "w_mid": w_mid, "b_mid": b_mid, "w_out": w_out, "b_out": b_out}


step_size = 0.15
stress_scale = 0.5
stress_pairs = ((0, 3, 4), (3, 1, 5), (4, 5, 2))
highest = lax.Precision.HIGHEST

def face_coefficients(viscosity):
    coeffs = []
    for dimension in range(3):
        forward_coeff = 0.5 * (viscosity + jnp.roll(viscosity, -1, dimension))
        backward_coeff = 0.5 * (viscosity + jnp.roll(viscosity, 1, dimension))
        coeffs.append((forward_coeff, backward_coeff))
    return coeffs

def diffuse(values, coeffs):
    flux_sum = jnp.zeros_like(values)
    for dimension in range(3):
        forward_coeff, backward_coeff = coeffs[dimension]
        leading = jnp.roll(values, -1, dimension + 1)
        trailing = jnp.roll(values, 1, dimension + 1)
        flux_sum = flux_sum + forward_coeff * (leading - values) - backward_coeff * (values - trailing)
    return values + step_size * flux_sum

def central(values, dimension):
    return 0.5 * (jnp.roll(values, -1, dimension) - jnp.roll(values, 1, dimension))

def divergence(derivatives):
    pieces = []
    for component in range(3):
        pairs = stress_pairs[component]
        pieces.append(derivatives[0][pairs[0]] + derivatives[1][pairs[1]] + derivatives[2][pairs[2]])
    return jnp.stack(pieces)

def closure(features, owners, params):
    w_in, b_in, w_mid, b_mid, w_out, b_out = params

    def plane_stress(pieces):
        plane_values, row_owner = pieces
        hidden_one = jnp.tanh(jnp.einsum('fyz,yfh->hyz', plane_values, w_in[row_owner], precision=highest) + b_in[row_owner].T[:, :, None])
        hidden_two = jnp.tanh(jnp.einsum('hyz,yhk->kyz', hidden_one, w_mid[row_owner], precision=highest) + b_mid[row_owner].T[:, :, None])
        return jnp.einsum('hyz,yho->oyz', hidden_two, w_out[row_owner], precision=highest) + b_out[row_owner].T[:, :, None]
    planes = jnp.moveaxis(features, 1, 0)
    stress = lax.map(jax.checkpoint(plane_stress), (planes, owners))
    return jnp.moveaxis(stress, 0, 1)

def reference(velocity, viscosity, cotangent, assignment, w_in, b_in, w_mid, b_mid, w_out, b_out):
    owners = assignment[:, 0].reshape(N_GX, N_YZ, CX, CY).transpose(0, 2, 1, 3).reshape(NX, NY)
    coeffs = face_coefficients(viscosity)

    def forward(start, params):
        velocity_now = start
        for substep in range(SUBSTEPS):
            velocity_now = diffuse(velocity_now, coeffs)
        features = jnp.stack([central(velocity_now, dimension + 1) for dimension in range(3)], axis=1).reshape(9, NX, NY, NZ)
        stress = closure(features, owners, params)
        derivatives = [central(stress, dimension + 1) for dimension in range(3)]
        return velocity_now - stress_scale * divergence(derivatives)
    params = (w_in, b_in, w_mid, b_mid, w_out, b_out)
    predicted, pullback = jax.vjp(forward, velocity, params)
    grad_velocity, weight_grads = pullback(cotangent)
    return (predicted, grad_velocity, weight_grads[0], weight_grads[1], weight_grads[2], weight_grads[3], weight_grads[4], weight_grads[5])
```

```python
import jax
import jax.numpy as jnp
from jax import lax
from jax.sharding import PartitionSpec as P

SUBSTEPS = 4
STEP = 0.15
SCALE = 0.5
CAP = 2
PREC = lax.Precision.HIGH
AXES = ("gx", "yz")


def permute(value, target):
    n_gx, n_yz = lax.axis_size("gx"), lax.axis_size("yz")
    pairs = []
    for g in range(n_gx):
        for y in range(n_yz):
            to_g, to_y = target(g, y)
            pairs.append((g * n_yz + y, (to_g % n_gx) * n_yz + to_y % n_yz))
    return lax.ppermute(value, AXES, pairs)


def to_partner(value):
    return permute(value, lambda g, y: (g ^ 1, y))


def to_outer(value, chips):
    return permute(value, lambda g, y: (g + 2 * chips if g % 2 == 0 else g - 2 * chips, y))


def packed(pieces):
    return jnp.concatenate([p.reshape(-1, 128) for p in pieces], axis=0)


def unpacked(buffer, shapes):
    pieces, at = [], 0
    for shape in shapes:
        rows = 1
        for n in shape[:-1]:
            rows *= n
        pieces.append(buffer[at : at + rows].reshape(shape))
        at += rows
    return pieces


def swap_y(low_pieces, high_pieces):
    shapes_low = [p.shape for p in low_pieces]
    shapes_high = [p.shape for p in high_pieces]
    below = permute(packed(low_pieces), lambda g, y: (g, y + 1))
    above = permute(packed(high_pieces), lambda g, y: (g, y - 1))
    return unpacked(below, shapes_low), unpacked(above, shapes_high)


def flux_step(values, visc):
    center, own = values[:, 1:-1, 1:-1], visc[1:-1, 1:-1]

    def part(next_value, prev_value, next_visc, prev_visc):
        return (0.5 * (own + next_visc)) * (next_value - center) - (0.5 * (own + prev_visc)) * (
            center - prev_value
        )

    flux = part(values[:, 2:, 1:-1], values[:, :-2, 1:-1], visc[2:, 1:-1], visc[:-2, 1:-1])
    flux = flux + part(values[:, 1:-1, 2:], values[:, 1:-1, :-2], visc[1:-1, 2:], visc[1:-1, :-2])
    flux = flux + part(
        jnp.roll(center, -1, 3), jnp.roll(center, 1, 3), jnp.roll(own, -1, 2), jnp.roll(own, 1, 2)
    )
    return center + STEP * flux


def along_z(values):
    return 0.5 * (jnp.roll(values, -1, -1) - jnp.roll(values, 1, -1))


def slots_of(owners):
    count = owners.shape[0]
    same = owners[:, None] == owners[None, :]
    earlier = jnp.arange(count)[None, :] < jnp.arange(count)[:, None]
    rank = jnp.sum((same & earlier).astype(jnp.int32), axis=1)
    return owners * CAP + rank


def local(velocity, viscosity, cotangent, assignment, w_in, b_in, w_mid, b_mid, w_out, b_out):
    experts = lax.axis_size("yz")
    core = lax.axis_index("gx") % 2
    sign = (1 - 2 * core).astype(jnp.float32)

    def mirror(v, dim):
        return jnp.where(core == 0, v, jnp.flip(v, dim))

    fields = jnp.concatenate([mirror(velocity, 1), mirror(viscosity, 0)[None]], axis=0)
    cot = mirror(cotangent, 1)
    owners = mirror(assignment.reshape(2, 8), 0).reshape(16)
    slot = slots_of(owners)

    (f_low, c_low), (f_high, c_high) = swap_y(
        [fields[:, :, 3:], cot[:, :, 7:]], [fields[:, :, :5], cot[:, :, :1]]
    )
    wide = jnp.concatenate([f_low, fields, f_high], axis=2)
    got = to_partner(packed([wide, cot]))
    partner, c_partner = unpacked(got, [wide.shape, cot.shape])
    chip = jnp.concatenate([wide, jnp.flip(partner, 1)], axis=1)
    near = to_outer(packed([chip[:, :, 1:17], c_partner[:, 0]]), 1)
    far = to_outer(chip[:, 3, 5:13], 2)
    outer, c_outer = unpacked(near, [(4, 4, 16, 128), (3, 8, 128)])
    inner = jnp.flip(to_partner(outer[:, 1:]), 1)
    pad_y = ((0, 0), (0, 0), (1, 1), (0, 0))
    block = jnp.concatenate(
        [
            jnp.pad(far[:, None], ((0, 0), (0, 0), (5, 5), (0, 0))),
            jnp.pad(outer, pad_y),
            chip,
            jnp.pad(inner, pad_y),
        ],
        axis=1,
    )
    state, visc = block[:3], block[3]
    for substep in range(SUBSTEPS):
        state = flux_step(state, visc)
        visc = visc[1:-1, 1:-1]
    own_state = state[:, 1:3, 1:9]
    feature_x = (0.5 * sign) * (state[:, 2:, 1:9] - state[:, :2, 1:9])
    feature_y = 0.5 * (state[:, 1:3, 2:] - state[:, 1:3, :8])
    features = jnp.stack([feature_x, feature_y, along_z(own_state)], axis=1)

    c_x = jnp.concatenate([c_outer[:, None], cot, c_partner[:, 1:]], axis=1)
    c_y = jnp.concatenate([c_low, cot, c_high], axis=2)
    d_x = (0.5 * sign) * (c_x[:, 2:] - c_x[:, :2])
    d_y = 0.5 * (c_y[:, :, 2:] - c_y[:, :, :-2])
    d_z = along_z(cot)
    stress_grad = SCALE * jnp.stack(
        [d_x[0], d_y[1], d_z[2], d_y[0] + d_x[1], d_z[0] + d_x[2], d_z[1] + d_y[2]]
    )

    columns = jnp.concatenate([features.reshape(9, 16, 128), stress_grad.reshape(6, 16, 128)], axis=0)
    by_slot = slot[None, :] == jnp.arange(experts * CAP, dtype=jnp.int32)[:, None]
    source = jnp.sum(jnp.where(by_slot, jnp.arange(16, dtype=jnp.int32)[None, :], 0), axis=1)
    occupied = jnp.any(by_slot, axis=1)
    send = jnp.where(occupied[:, None, None], jnp.transpose(columns, (1, 0, 2))[source], 0.0)
    send = send.reshape(experts, CAP * 15, 128)
    recv = lax.all_to_all(send, "yz", 0, 0, tiled=True).reshape(experts * CAP, 15, 128)

    w1, w2, w3 = w_in[0], w_mid[0], w_out[0]
    x = jnp.transpose(recv[:, :9], (1, 0, 2)).reshape(9, -1)
    sg = jnp.transpose(recv[:, 9:], (1, 0, 2)).reshape(6, -1)

    def dot(a, b, ca, cb):
        return lax.dot_general(a, b, (((ca,), (cb,)), ((), ())), precision=PREC)

    h1 = jnp.tanh(dot(w1, x, 0, 0) + b_in[0][:, None])
    h2 = jnp.tanh(dot(w2, h1, 0, 0) + b_mid[0][:, None])
    stress = dot(w3, h2, 0, 0) + b_out[0][:, None]
    g2 = dot(w3, sg, 1, 0) * (1.0 - h2 * h2)
    g1 = dot(w2, g2, 1, 0) * (1.0 - h1 * h1)
    fg = dot(w1, g1, 1, 0)
    grads = [
        dot(x, g1, 1, 1),
        jnp.sum(g1, axis=1)[None],
        dot(h1, g2, 1, 1),
        jnp.sum(g2, axis=1)[None],
        dot(sg, h2, 1, 1),
        jnp.pad(jnp.sum(sg, axis=1), (0, 122))[None],
    ]

    back = jnp.concatenate([fg, stress], axis=0).reshape(15, experts * CAP, 128)
    back = jnp.transpose(back, (1, 0, 2)).reshape(experts, CAP * 15, 128)
    home = lax.all_to_all(back, "yz", 0, 0, tiled=True).reshape(experts * CAP, 15, 128)
    home = jnp.transpose(home[slot], (1, 0, 2)).reshape(15, 2, 8, 128)

    chips = lax.axis_size("gx") // 2
    vector = jnp.concatenate(grads, axis=0)
    chunk = -(-vector.shape[0] // chips)
    vector = vector + to_partner(vector)
    split = jnp.pad(vector, ((0, chunk * chips - vector.shape[0]), (0, 0))).reshape(chips, chunk, 128)
    groups = [list(range(0, 2 * chips, 2)), list(range(1, 2 * chips, 2))]
    parts = lax.all_to_all(split, "gx", 0, 0, axis_index_groups=groups, tiled=True)
    mine = jnp.sum(parts, axis=0)
    whole = lax.all_to_all(
        jnp.broadcast_to(mine, split.shape), "gx", 0, 0, axis_index_groups=groups, tiled=True
    ).reshape(-1, 128)

    fgrad = home[:9].reshape(3, 3, 2, 8, 128)
    fx, fy, fz = fgrad[:, 0], fgrad[:, 1], fgrad[:, 2]
    tau = home[9:]
    tau_x = jnp.stack([tau[0], tau[3], tau[4]])
    tau_y = jnp.stack([tau[3], tau[1], tau[5]])
    tau_z = jnp.stack([tau[4], tau[5], tau[2]])
    part = cot - along_z(fz)
    (p_low, x_low, y_low, t_low), (p_high, x_high, y_high, t_high) = swap_y(
        [part[:, :, 4:], fx[:, :, 4:], fy[:, :, 3:], tau_y[:, :, 7:]],
        [part[:, :, :4], fx[:, :, :4], fy[:, :, :5], tau_y[:, :, :1]],
    )
    fy_wide = jnp.concatenate([y_low, fy, y_high], axis=2)
    part = jnp.concatenate([p_low, part, p_high], axis=2)
    part = part - 0.5 * (fy_wide[:, :, 2:] - fy_wide[:, :, :-2])
    fx_wide = jnp.concatenate([x_low, fx, x_high], axis=2)
    got = to_partner(packed([part, fx_wide, tau_x]))
    part_other, fx_other, tau_other = unpacked(got, [part.shape, fx_wide.shape, tau_x.shape])
    part_chip = jnp.concatenate([part, jnp.flip(part_other, 1)], axis=1)
    fx_chip = jnp.concatenate([fx_wide, jnp.flip(fx_other, 1)], axis=1)
    half = 0.5 * sign
    zero = jnp.zeros_like(fx_chip[:, :1])
    fx_pad = jnp.concatenate([zero, fx_chip, zero], axis=1)
    adj_chip = part_chip - half * (fx_pad[:, 2:] - fx_pad[:, :-2])
    near = to_outer(packed([adj_chip, fx_chip[:, 3], tau_other[:, 0]]), 1)
    far = to_outer(fx_chip[:, 3, 4:12], 2)
    adj_outer, fx_outer, tau_outer = unpacked(near, [(3, 4, 16, 128), (3, 16, 128), (3, 8, 128)])
    far = jnp.pad(far, ((0, 0), (4, 4), (0, 0)))
    adj_outer = jnp.concatenate(
        [
            adj_outer[:, :1] + half * far[:, None],
            adj_outer[:, 1:3],
            adj_outer[:, 3:] - half * fx_chip[:, :1],
        ],
        axis=1,
    )
    got = to_partner(packed([adj_outer[:, 2:], fx_outer]))
    adj_inner, fx_inner = unpacked(got, [(3, 2, 16, 128), (3, 16, 128)])
    adjoint = jnp.concatenate(
        [
            adj_outer,
            adj_chip[:, :1] + half * fx_outer[:, None],
            adj_chip[:, 1:3],
            adj_chip[:, 3:] - half * fx_inner[:, None],
            jnp.flip(adj_inner, 1),
        ],
        axis=1,
    )
    visc = block[3, 1:-1, 1:-1]
    for substep in range(SUBSTEPS):
        adjoint = flux_step(adjoint, visc)
        visc = visc[1:-1, 1:-1]

    t_x = jnp.concatenate([tau_outer[:, None], tau_x, tau_other[:, 1:]], axis=1)
    t_y = jnp.concatenate([t_low, tau_y, t_high], axis=2)
    predicted = own_state - SCALE * (
        half * (t_x[:, 2:] - t_x[:, :2]) + 0.5 * (t_y[:, :, 2:] - t_y[:, :, :-2]) + along_z(tau_z)
    )
    return (
        mirror(predicted, 1),
        mirror(adjoint, 1),
        whole[None, 0:9],
        whole[None, 9],
        whole[None, 10:138],
        whole[None, 138],
        jnp.transpose(whole[139:145])[None],
        whole[None, 145, :6],
    )


def solution(mesh):
    placed = (
        P(None, "gx", "yz", None),
        P("gx", "yz", None),
        P(None, "gx", "yz", None),
        P(("gx", "yz"), None),
        P("yz", None, None),
        P("yz", None),
        P("yz", None, None),
        P("yz", None),
        P("yz", None, None),
        P("yz", None),
    )
    return jax.shard_map(
        local,
        mesh=mesh,
        in_specs=placed,
        out_specs=(
            P(None, "gx", "yz", None),
            P(None, "gx", "yz", None),
            P("yz", None, None),
            P("yz", None),
            P("yz", None, None),
            P("yz", None),
            P("yz", None, None),
            P("yz", None),
        ),
        check_vma=False,
    )
```

```python
import jax
import jax.numpy as jnp
from jax import lax
from jax.sharding import PartitionSpec as P

SUBSTEPS = 4
STEP = 0.15
SCALE = 0.5
CAP = 2
PREC = lax.Precision.HIGH
AXES = ("gx", "yz")


def permute(value, target):
    n_gx, n_yz = lax.axis_size("gx"), lax.axis_size("yz")
    pairs = []
    for g in range(n_gx):
        for y in range(n_yz):
            to_g, to_y = target(g, y)
            pairs.append((g * n_yz + y, (to_g % n_gx) * n_yz + to_y % n_yz))
    return lax.ppermute(value, AXES, pairs)


def exchange(value, axis, groups=None):
    return lax.all_to_all(value, axis, 0, 0, axis_index_groups=groups, tiled=True)


def to_partner(value):
    return permute(value, lambda g, y: (g ^ 1, y))


def to_outer(value, chips):
    return permute(value, lambda g, y: (g + 2 * chips if g % 2 == 0 else g - 2 * chips, y))


def packed(pieces):
    return jnp.concatenate([p.reshape(-1, 128) for p in pieces], axis=0)


def unpacked(buffer, shapes):
    pieces, at = [], 0
    for shape in shapes:
        rows = 1
        for n in shape[:-1]:
            rows *= n
        pieces.append(buffer[at : at + rows].reshape(shape))
        at += rows
    return pieces


def swap_y(low_pieces, high_pieces):
    shapes_low = [p.shape for p in low_pieces]
    shapes_high = [p.shape for p in high_pieces]
    below = permute(packed(low_pieces), lambda g, y: (g, y + 1))
    above = permute(packed(high_pieces), lambda g, y: (g, y - 1))
    return unpacked(below, shapes_low), unpacked(above, shapes_high)


def flux_step(values, visc):
    center, own = values[:, 1:-1, 1:-1], visc[1:-1, 1:-1]

    def part(next_value, prev_value, next_visc, prev_visc):
        return (0.5 * (own + next_visc)) * (next_value - center) - (0.5 * (own + prev_visc)) * (
            center - prev_value
        )

    flux = part(values[:, 2:, 1:-1], values[:, :-2, 1:-1], visc[2:, 1:-1], visc[:-2, 1:-1])
    flux = flux + part(values[:, 1:-1, 2:], values[:, 1:-1, :-2], visc[1:-1, 2:], visc[1:-1, :-2])
    flux = flux + part(
        jnp.roll(center, -1, 3), jnp.roll(center, 1, 3), jnp.roll(own, -1, 2), jnp.roll(own, 1, 2)
    )
    return center + STEP * flux


def along_z(values):
    return 0.5 * (jnp.roll(values, -1, -1) - jnp.roll(values, 1, -1))


def slots_of(owners):
    count = owners.shape[0]
    same = owners[:, None] == owners[None, :]
    earlier = jnp.arange(count)[None, :] < jnp.arange(count)[:, None]
    rank = jnp.sum((same & earlier).astype(jnp.int32), axis=1)
    return owners * CAP + rank


def step(velocity, viscosity, cotangent, assignment, w_in, b_in, w_mid, b_mid, w_out, b_out):
    experts = lax.axis_size("yz")
    core = lax.axis_index("gx") % 2
    sign = (1 - 2 * core).astype(jnp.float32)

    def mirror(v, dim):
        return jnp.where(core == 0, v, jnp.flip(v, dim))

    fields = jnp.concatenate([mirror(velocity, 1), mirror(viscosity, 0)[None]], axis=0)
    cot = mirror(cotangent, 1)
    owners = mirror(assignment.reshape(2, 8), 0).reshape(16)
    slot = slots_of(owners)

    (f_low, c_low), (f_high, c_high) = swap_y(
        [fields[:, :, 3:], cot[:, :, 7:]], [fields[:, :, :5], cot[:, :, :1]]
    )
    wide = jnp.concatenate([f_low, fields, f_high], axis=2)
    got = to_partner(packed([wide, cot]))
    partner, c_partner = unpacked(got, [wide.shape, cot.shape])
    chip = jnp.concatenate([wide, jnp.flip(partner, 1)], axis=1)
    near = to_outer(packed([chip[:, :, 1:17], c_partner[:, 0]]), 1)
    far = to_outer(chip[:, 3, 5:13], 2)
    outer, c_outer = unpacked(near, [(4, 4, 16, 128), (3, 8, 128)])
    inner = jnp.flip(to_partner(outer[:, 1:]), 1)
    pad_y = ((0, 0), (0, 0), (1, 1), (0, 0))
    block = jnp.concatenate(
        [
            jnp.pad(far[:, None], ((0, 0), (0, 0), (5, 5), (0, 0))),
            jnp.pad(outer, pad_y),
            chip,
            jnp.pad(inner, pad_y),
        ],
        axis=1,
    )
    state, visc = block[:3], block[3]
    for _ in range(SUBSTEPS):
        state = flux_step(state, visc)
        visc = visc[1:-1, 1:-1]
    own_state = state[:, 1:3, 1:9]
    feature_x = (0.5 * sign) * (state[:, 2:, 1:9] - state[:, :2, 1:9])
    feature_y = 0.5 * (state[:, 1:3, 2:] - state[:, 1:3, :8])
    features = jnp.stack([feature_x, feature_y, along_z(own_state)], axis=1)

    c_x = jnp.concatenate([c_outer[:, None], cot, c_partner[:, 1:]], axis=1)
    c_y = jnp.concatenate([c_low, cot, c_high], axis=2)
    d_x = (0.5 * sign) * (c_x[:, 2:] - c_x[:, :2])
    d_y = 0.5 * (c_y[:, :, 2:] - c_y[:, :, :-2])
    d_z = along_z(cot)
    stress_grad = SCALE * jnp.stack(
        [d_x[0], d_y[1], d_z[2], d_y[0] + d_x[1], d_z[0] + d_x[2], d_z[1] + d_y[2]]
    )

    columns = jnp.concatenate([features.reshape(9, 16, 128), stress_grad.reshape(6, 16, 128)], axis=0)
    by_slot = slot[None, :] == jnp.arange(experts * CAP, dtype=jnp.int32)[:, None]
    source = jnp.sum(jnp.where(by_slot, jnp.arange(16, dtype=jnp.int32)[None, :], 0), axis=1)
    occupied = jnp.any(by_slot, axis=1)
    send = jnp.where(occupied[:, None, None], jnp.transpose(columns, (1, 0, 2))[source], 0.0)
    send = send.reshape(experts, CAP * 15, 128)
    recv = exchange(send, "yz").reshape(experts * CAP, 15, 128)

    w1, w2, w3 = w_in[0], w_mid[0], w_out[0]
    x = jnp.transpose(recv[:, :9], (1, 0, 2)).reshape(9, -1)
    sg = jnp.transpose(recv[:, 9:], (1, 0, 2)).reshape(6, -1)

    def dot(a, b, ca, cb):
        return lax.dot_general(a, b, (((ca,), (cb,)), ((), ())), precision=PREC)

    h1 = jnp.tanh(dot(w1, x, 0, 0) + b_in[0][:, None])
    h2 = jnp.tanh(dot(w2, h1, 0, 0) + b_mid[0][:, None])
    stress = dot(w3, h2, 0, 0) + b_out[0][:, None]
    g2 = dot(w3, sg, 1, 0) * (1.0 - h2 * h2)
    g1 = dot(w2, g2, 1, 0) * (1.0 - h1 * h1)
    fg = dot(w1, g1, 1, 0)
    grads = [
        dot(x, g1, 1, 1),
        jnp.sum(g1, axis=1)[None],
        dot(h1, g2, 1, 1),
        jnp.sum(g2, axis=1)[None],
        dot(sg, h2, 1, 1),
        jnp.pad(jnp.sum(sg, axis=1), (0, 122))[None],
    ]

    back = jnp.concatenate([fg, stress], axis=0).reshape(15, experts * CAP, 128)
    back = jnp.transpose(back, (1, 0, 2)).reshape(experts, CAP * 15, 128)
    home = exchange(back, "yz").reshape(experts * CAP, 15, 128)
    home = jnp.transpose(home[slot], (1, 0, 2)).reshape(15, 2, 8, 128)

    chips = lax.axis_size("gx") // 2
    vector = jnp.concatenate(grads, axis=0)
    chunk = -(-vector.shape[0] // chips)
    vector = vector + to_partner(vector)
    split = jnp.pad(vector, ((0, chunk * chips - vector.shape[0]), (0, 0))).reshape(chips, chunk, 128)
    groups = [list(range(0, 2 * chips, 2)), list(range(1, 2 * chips, 2))]
    split, home = lax.optimization_barrier((split, home))
    parts = exchange(split, "gx", groups)
    mine = jnp.sum(parts, axis=0)
    whole = exchange(jnp.broadcast_to(mine, split.shape), "gx", groups).reshape(-1, 128)

    fgrad = home[:9].reshape(3, 3, 2, 8, 128)
    fx, fy, fz = fgrad[:, 0], fgrad[:, 1], fgrad[:, 2]
    tau = home[9:]
    tau_x = jnp.stack([tau[0], tau[3], tau[4]])
    tau_y = jnp.stack([tau[3], tau[1], tau[5]])
    tau_z = jnp.stack([tau[4], tau[5], tau[2]])
    part = cot - along_z(fz)
    (p_low, x_low, y_low, t_low), (p_high, x_high, y_high, t_high) = swap_y(
        [part[:, :, 4:], fx[:, :, 4:], fy[:, :, 3:], tau_y[:, :, 7:]],
        [part[:, :, :4], fx[:, :, :4], fy[:, :, :5], tau_y[:, :, :1]],
    )
    fy_wide = jnp.concatenate([y_low, fy, y_high], axis=2)
    part = jnp.concatenate([p_low, part, p_high], axis=2)
    part = part - 0.5 * (fy_wide[:, :, 2:] - fy_wide[:, :, :-2])
    fx_wide = jnp.concatenate([x_low, fx, x_high], axis=2)
    got = to_partner(packed([part, fx_wide, tau_x]))
    part_other, fx_other, tau_other = unpacked(got, [part.shape, fx_wide.shape, tau_x.shape])
    part_chip = jnp.concatenate([part, jnp.flip(part_other, 1)], axis=1)
    fx_chip = jnp.concatenate([fx_wide, jnp.flip(fx_other, 1)], axis=1)
    half = 0.5 * sign
    zero = jnp.zeros_like(fx_chip[:, :1])
    fx_pad = jnp.concatenate([zero, fx_chip, zero], axis=1)
    adj_chip = part_chip - half * (fx_pad[:, 2:] - fx_pad[:, :-2])
    near = to_outer(packed([adj_chip, fx_chip[:, 3], tau_other[:, 0]]), 1)
    far = to_outer(fx_chip[:, 3, 4:12], 2)
    adj_outer, fx_outer, tau_outer = unpacked(near, [(3, 4, 16, 128), (3, 16, 128), (3, 8, 128)])
    far = jnp.pad(far, ((0, 0), (4, 4), (0, 0)))
    adj_outer = jnp.concatenate(
        [
            adj_outer[:, :1] + half * far[:, None],
            adj_outer[:, 1:3],
            adj_outer[:, 3:] - half * fx_chip[:, :1],
        ],
        axis=1,
    )
    got = to_partner(packed([adj_outer[:, 2:], fx_outer]))
    adj_inner, fx_inner = unpacked(got, [(3, 2, 16, 128), (3, 16, 128)])
    adjoint = jnp.concatenate(
        [
            adj_outer,
            adj_chip[:, :1] + half * fx_outer[:, None],
            adj_chip[:, 1:3],
            adj_chip[:, 3:] - half * fx_inner[:, None],
            jnp.flip(adj_inner, 1),
        ],
        axis=1,
    )
    visc = block[3, 1:-1, 1:-1]
    for _ in range(SUBSTEPS):
        adjoint = flux_step(adjoint, visc)
        visc = visc[1:-1, 1:-1]

    t_x = jnp.concatenate([tau_outer[:, None], tau_x, tau_other[:, 1:]], axis=1)
    t_y = jnp.concatenate([t_low, tau_y, t_high], axis=2)
    predicted = own_state - SCALE * (
        half * (t_x[:, 2:] - t_x[:, :2]) + 0.5 * (t_y[:, :, 2:] - t_y[:, :, :-2]) + along_z(tau_z)
    )
    return (
        mirror(predicted, 1),
        mirror(adjoint, 1),
        whole[None, 0:9],
        whole[None, 9],
        whole[None, 10:138],
        whole[None, 138],
        jnp.transpose(whole[139:145])[None],
        whole[None, 145, :6],
    )


def solution(mesh):
    placed = (
        P(None, "gx", "yz", None),
        P("gx", "yz", None),
        P(None, "gx", "yz", None),
        P(("gx", "yz"), None),
        P("yz", None, None),
        P("yz", None),
        P("yz", None, None),
        P("yz", None),
        P("yz", None, None),
        P("yz", None),
    )
    return jax.shard_map(
        step,
        mesh=mesh,
        in_specs=placed,
        out_specs=(
            P(None, "gx", "yz", None),
            P(None, "gx", "yz", None),
            P("yz", None, None),
            P("yz", None),
            P("yz", None, None),
            P("yz", None),
            P("yz", None, None),
            P("yz", None),
        ),
        check_vma=False,
    )
```

```python
import jax
import jax.numpy as jnp
from jax import lax
from jax.sharding import PartitionSpec as P

SUBSTEPS = 4
STEP = 0.15
SCALE = 0.5
CAP = 2
PREC = lax.Precision.HIGH
AXES = ("gx", "yz")


def permute(value, target):
    n_gx, n_yz = lax.axis_size("gx"), lax.axis_size("yz")
    pairs = []
    for g in range(n_gx):
        for y in range(n_yz):
            to_g, to_y = target(g, y)
            pairs.append((g * n_yz + y, (to_g % n_gx) * n_yz + to_y % n_yz))
    return lax.ppermute(value, AXES, pairs)


def exchange(value, axis, groups=None):
    return lax.all_to_all(value, axis, 0, 0, axis_index_groups=groups, tiled=True)


def to_partner(value):
    return permute(value, lambda g, y: (g ^ 1, y))


def across(value):
    return permute(value, lambda g, y: (g - 1 if g % 2 == 0 else g + 1, y))


def packed(pieces):
    return jnp.concatenate([p.reshape(-1, 128) for p in pieces], axis=0)


def unpacked(buffer, shapes):
    pieces, at = [], 0
    for shape in shapes:
        rows = 1
        for n in shape[:-1]:
            rows *= n
        pieces.append(buffer[at : at + rows].reshape(shape))
        at += rows
    return pieces


def swap_y(low_pieces, high_pieces):
    shapes_low = [p.shape for p in low_pieces]
    shapes_high = [p.shape for p in high_pieces]
    below = permute(packed(low_pieces), lambda g, y: (g, y + 1))
    above = permute(packed(high_pieces), lambda g, y: (g, y - 1))
    return unpacked(below, shapes_low), unpacked(above, shapes_high)


def flux_step(values, visc):
    center, own = values[:, 1:-1, 1:-1], visc[1:-1, 1:-1]

    def part(next_value, prev_value, next_visc, prev_visc):
        return (0.5 * (own + next_visc)) * (next_value - center) - (0.5 * (own + prev_visc)) * (
            center - prev_value
        )

    flux = part(values[:, 2:, 1:-1], values[:, :-2, 1:-1], visc[2:, 1:-1], visc[:-2, 1:-1])
    flux = flux + part(values[:, 1:-1, 2:], values[:, 1:-1, :-2], visc[1:-1, 2:], visc[1:-1, :-2])
    flux = flux + part(
        jnp.roll(center, -1, 3), jnp.roll(center, 1, 3), jnp.roll(own, -1, 2), jnp.roll(own, 1, 2)
    )
    return center + STEP * flux


def along_z(values):
    return 0.5 * (jnp.roll(values, -1, -1) - jnp.roll(values, 1, -1))


def slots_of(owners):
    count = owners.shape[0]
    same = owners[:, None] == owners[None, :]
    earlier = jnp.arange(count)[None, :] < jnp.arange(count)[:, None]
    rank = jnp.sum((same & earlier).astype(jnp.int32), axis=1)
    return owners * CAP + rank


def step(velocity, viscosity, cotangent, assignment, w_in, b_in, w_mid, b_mid, w_out, b_out):
    experts = lax.axis_size("yz")
    core = lax.axis_index("gx") % 2
    sign = (1 - 2 * core).astype(jnp.float32)

    def mirror(v, dim):
        return jnp.where(core == 0, v, jnp.flip(v, dim))

    fields = jnp.concatenate([mirror(velocity, 1), mirror(viscosity, 0)[None]], axis=0)
    cot = mirror(cotangent, 1)
    owners = mirror(assignment.reshape(2, 8), 0).reshape(16)
    slot = slots_of(owners)

    (f_low, c_low), (f_high, c_high) = swap_y(
        [fields[:, :, 3:], cot[:, :, 7:]], [fields[:, :, :5], cot[:, :, :1]]
    )
    wide = jnp.concatenate([f_low, fields, f_high], axis=2)
    got = across(packed([fields[:, 0], cot[:, 0]]))
    f_edge, c_edge = unpacked(got, [(4, 8, 128), (3, 8, 128)])
    got = to_partner(packed([wide, f_edge, cot[:, 1]]))
    partner, partner_edge, c_partner = unpacked(got, [wide.shape, (4, 8, 128), (3, 8, 128)])
    chip = jnp.concatenate([wide, jnp.flip(partner, 1)], axis=1)
    got = across(packed([chip[:, :, 1:17], partner_edge]))
    outer, far = unpacked(got, [(4, 4, 16, 128), (4, 8, 128)])
    outer = jnp.flip(outer, 1)
    inner = jnp.flip(to_partner(outer[:, 1:]), 1)
    pad_y = ((0, 0), (0, 0), (1, 1), (0, 0))
    block = jnp.concatenate(
        [
            jnp.pad(far[:, None], ((0, 0), (0, 0), (5, 5), (0, 0))),
            jnp.pad(outer, pad_y),
            chip,
            jnp.pad(inner, pad_y),
        ],
        axis=1,
    )
    state, visc = block[:3], block[3]
    for _ in range(SUBSTEPS):
        state = flux_step(state, visc)
        visc = visc[1:-1, 1:-1]
    own_state = state[:, 1:3, 1:9]
    feature_x = (0.5 * sign) * (state[:, 2:, 1:9] - state[:, :2, 1:9])
    feature_y = 0.5 * (state[:, 1:3, 2:] - state[:, 1:3, :8])
    features = jnp.stack([feature_x, feature_y, along_z(own_state)], axis=1)

    c_x = jnp.concatenate([c_edge[:, None], cot, c_partner[:, None]], axis=1)
    c_y = jnp.concatenate([c_low, cot, c_high], axis=2)
    d_x = (0.5 * sign) * (c_x[:, 2:] - c_x[:, :2])
    d_y = 0.5 * (c_y[:, :, 2:] - c_y[:, :, :-2])
    d_z = along_z(cot)
    stress_grad = SCALE * jnp.stack(
        [d_x[0], d_y[1], d_z[2], d_y[0] + d_x[1], d_z[0] + d_x[2], d_z[1] + d_y[2]]
    )

    columns = jnp.concatenate([features.reshape(9, 16, 128), stress_grad.reshape(6, 16, 128)], axis=0)
    by_slot = slot[None, :] == jnp.arange(experts * CAP, dtype=jnp.int32)[:, None]
    source = jnp.sum(jnp.where(by_slot, jnp.arange(16, dtype=jnp.int32)[None, :], 0), axis=1)
    occupied = jnp.any(by_slot, axis=1)
    send = jnp.where(occupied[:, None, None], jnp.transpose(columns, (1, 0, 2))[source], 0.0)
    send = send.reshape(experts, CAP * 15, 128)
    recv = exchange(send, "yz").reshape(experts * CAP, 15, 128)

    w1, w2, w3 = w_in[0], w_mid[0], w_out[0]
    x = jnp.transpose(recv[:, :9], (1, 0, 2)).reshape(9, -1)
    sg = jnp.transpose(recv[:, 9:], (1, 0, 2)).reshape(6, -1)

    def dot(a, b, ca, cb):
        return lax.dot_general(a, b, (((ca,), (cb,)), ((), ())), precision=PREC)

    h1 = jnp.tanh(dot(w1, x, 0, 0) + b_in[0][:, None])
    h2 = jnp.tanh(dot(w2, h1, 0, 0) + b_mid[0][:, None])
    stress = dot(w3, h2, 0, 0) + b_out[0][:, None]
    g2 = dot(w3, sg, 1, 0) * (1.0 - h2 * h2)
    g1 = dot(w2, g2, 1, 0) * (1.0 - h1 * h1)
    fg = dot(w1, g1, 1, 0)
    grads = [
        dot(x, g1, 1, 1),
        jnp.sum(g1, axis=1)[None],
        dot(h1, g2, 1, 1),
        jnp.sum(g2, axis=1)[None],
        dot(sg, h2, 1, 1),
        jnp.pad(jnp.sum(sg, axis=1), (0, 122))[None],
    ]

    back = jnp.concatenate([fg, stress], axis=0).reshape(15, experts * CAP, 128)
    back = jnp.transpose(back, (1, 0, 2)).reshape(experts, CAP * 15, 128)
    home = exchange(back, "yz").reshape(experts * CAP, 15, 128)
    home = jnp.transpose(home[slot], (1, 0, 2)).reshape(15, 2, 8, 128)

    chips = lax.axis_size("gx") // 2
    vector = jnp.concatenate(grads, axis=0)
    chunk = -(-vector.shape[0] // chips)
    vector = vector + to_partner(vector)
    split = jnp.pad(vector, ((0, chunk * chips - vector.shape[0]), (0, 0))).reshape(chips, chunk, 128)
    groups = [list(range(0, 2 * chips, 2)), list(range(1, 2 * chips, 2))]
    parts = exchange(split, "gx", groups)
    mine = jnp.sum(parts, axis=0)
    whole = exchange(jnp.broadcast_to(mine, split.shape), "gx", groups).reshape(-1, 128)

    fgrad = home[:9].reshape(3, 3, 2, 8, 128)
    fx, fy, fz = fgrad[:, 0], fgrad[:, 1], fgrad[:, 2]
    tau = home[9:]
    tau_x = jnp.stack([tau[0], tau[3], tau[4]])
    tau_y = jnp.stack([tau[3], tau[1], tau[5]])
    tau_z = jnp.stack([tau[4], tau[5], tau[2]])
    part = cot - along_z(fz)
    (p_low, x_low, y_low, t_low), (p_high, x_high, y_high, t_high) = swap_y(
        [part[:, :, 4:], fx[:, :, 4:], fy[:, :, 3:], tau_y[:, :, 7:]],
        [part[:, :, :4], fx[:, :, :4], fy[:, :, :5], tau_y[:, :, :1]],
    )
    fy_wide = jnp.concatenate([y_low, fy, y_high], axis=2)
    part = jnp.concatenate([p_low, part, p_high], axis=2)
    part = part - 0.5 * (fy_wide[:, :, 2:] - fy_wide[:, :, :-2])
    fx_wide = jnp.concatenate([x_low, fx, x_high], axis=2)
    got = across(packed([fx[:, 0], tau_x[:, 0]]))
    fx_edge, tau_outer = unpacked(got, [(3, 8, 128), (3, 8, 128)])
    got = to_partner(packed([part, fx_wide, fx_edge, tau_x[:, 1]]))
    part_other, fx_other, fx_far, tau_other = unpacked(
        got, [part.shape, fx_wide.shape, (3, 8, 128), (3, 8, 128)]
    )
    part_chip = jnp.concatenate([part, jnp.flip(part_other, 1)], axis=1)
    fx_chip = jnp.concatenate([fx_wide, jnp.flip(fx_other, 1)], axis=1)
    half = 0.5 * sign
    zero = jnp.zeros_like(fx_chip[:, :1])
    fx_pad = jnp.concatenate([zero, fx_chip, zero], axis=1)
    adj_chip = part_chip - half * (fx_pad[:, 2:] - fx_pad[:, :-2])
    last = adj_chip[:, 3] - half * jnp.pad(fx_far, ((0, 0), (4, 4), (0, 0)))
    send = jnp.concatenate([adj_chip[:, :3], last[:, None]], axis=1)
    got = across(packed([send, fx_chip[:, 0]]))
    adj_outer, fx_outer = unpacked(got, [(3, 4, 16, 128), (3, 16, 128)])
    adj_outer = jnp.flip(adj_outer, 1)
    adj_outer = jnp.concatenate(
        [adj_outer[:, :3], adj_outer[:, 3:] - half * fx_chip[:, :1]], axis=1
    )
    got = to_partner(packed([adj_outer[:, 2:], fx_outer]))
    adj_inner, fx_inner = unpacked(got, [(3, 2, 16, 128), (3, 16, 128)])
    adjoint = jnp.concatenate(
        [
            adj_outer,
            adj_chip[:, :1] + half * fx_outer[:, None],
            adj_chip[:, 1:3],
            adj_chip[:, 3:] - half * fx_inner[:, None],
            jnp.flip(adj_inner, 1),
        ],
        axis=1,
    )
    visc = block[3, 1:-1, 1:-1]
    for _ in range(SUBSTEPS):
        adjoint = flux_step(adjoint, visc)
        visc = visc[1:-1, 1:-1]

    t_x = jnp.concatenate([tau_outer[:, None], tau_x, tau_other[:, None]], axis=1)
    t_y = jnp.concatenate([t_low, tau_y, t_high], axis=2)
    predicted = own_state - SCALE * (
        half * (t_x[:, 2:] - t_x[:, :2]) + 0.5 * (t_y[:, :, 2:] - t_y[:, :, :-2]) + along_z(tau_z)
    )
    return (
        mirror(predicted, 1),
        mirror(adjoint, 1),
        whole[None, 0:9],
        whole[None, 9],
        whole[None, 10:138],
        whole[None, 138],
        jnp.transpose(whole[139:145])[None],
        whole[None, 145, :6],
    )


def solution(mesh):
    placed = (
        P(None, "gx", "yz", None),
        P("gx", "yz", None),
        P(None, "gx", "yz", None),
        P(("gx", "yz"), None),
        P("yz", None, None),
        P("yz", None),
        P("yz", None, None),
        P("yz", None),
        P("yz", None, None),
        P("yz", None),
    )
    return jax.shard_map(
        step,
        mesh=mesh,
        in_specs=placed,
        out_specs=(
            P(None, "gx", "yz", None),
            P(None, "gx", "yz", None),
            P("yz", None, None),
            P("yz", None),
            P("yz", None, None),
            P("yz", None),
            P("yz", None, None),
            P("yz", None),
        ),
        check_vma=False,
    )
```

```python
import jax
import jax.numpy as jnp
from jax import lax
from jax.experimental import pallas as pl
from jax.experimental.pallas import tpu as pltpu
from jax.sharding import PartitionSpec as P

SUBSTEPS = 4
STEP = 0.15
SCALE = 0.5
CAP = 2
PREC = lax.Precision.HIGH
AXES = ("gx", "yz")
INTERPRET = False


def permute(value, target):
    n_gx, n_yz = lax.axis_size("gx"), lax.axis_size("yz")
    pairs = []
    for g in range(n_gx):
        for y in range(n_yz):
            to_g, to_y = target(g, y)
            pairs.append((g * n_yz + y, (to_g % n_gx) * n_yz + to_y % n_yz))
    return lax.ppermute(value, AXES, pairs)


def exchange(value, axis, groups=None):
    return lax.all_to_all(value, axis, 0, 0, axis_index_groups=groups, tiled=True)


def to_partner(value):
    return permute(value, lambda g, y: (g ^ 1, y))


def across(value):
    return permute(value, lambda g, y: (g - 1 if g % 2 == 0 else g + 1, y))


def packed(pieces):
    return jnp.concatenate([p.reshape(-1, 128) for p in pieces], axis=0)


def unpacked(buffer, shapes):
    pieces, at = [], 0
    for shape in shapes:
        rows = 1
        for n in shape[:-1]:
            rows *= n
        pieces.append(buffer[at : at + rows].reshape(shape))
        at += rows
    return pieces


def swap_y(low, high):
    below = permute(low, lambda g, y: (g, y + 1))
    above = permute(high, lambda g, y: (g, y - 1))
    return below, above


def spec(space):
    return pl.BlockSpec(memory_space=space)


def call(kernel, outs, scratch, smem_ins, args, smem_outs=()):
    return pl.pallas_call(
        kernel,
        out_shape=[jax.ShapeDtypeStruct(shape, dtype) for shape, dtype in outs],
        in_specs=[spec(pltpu.SMEM if i in smem_ins else pltpu.VMEM) for i in range(len(args))],
        out_specs=[spec(pltpu.SMEM if i in smem_outs else pltpu.VMEM) for i in range(len(outs))],
        scratch_shapes=scratch,
        interpret=INTERPRET,
    )(*args)


def turned(value, shift, axis):
    return pltpu.roll(value, shift % value.shape[axis], axis)


def coefficients(visc, rows, kx, ky, kz):
    for i in range(rows):
        own = visc[i]
        ky[i] = 0.5 * (own + turned(own, -1, 0))
        kz[i] = 0.5 * (own + turned(own, -1, 1))
        if i + 1 < rows:
            kx[i] = 0.5 * (own + visc[i + 1])


def diffusion(state, other, first, last, k_at, kx, ky, kz):
    for _ in range(SUBSTEPS):
        first, last = first + 1, last - 1
        for c in range(3):
            center = state[c, first]
            below = kx[k_at + first - 1] * (center - state[c, first - 1])
            for i in range(first, last + 1):
                k = k_at + i
                upper = state[c, i + 1]
                above = kx[k] * (upper - center)
                y_flux = ky[k] * (turned(center, -1, 0) - center)
                z_flux = kz[k] * (turned(center, -1, 1) - center)
                total = (above - below) + (y_flux - turned(y_flux, 1, 0))
                total = total + (z_flux - turned(z_flux, 1, 1))
                other[c, i] = center + STEP * total
                below, center = above, upper
        state, other = other, state
    return state


def forward_kernel(
    core_ref, owner_ref, fields, cot, low, high, edge, mate, near, mate_in,
    send, own_state, visc, slot_ref,
    work, spare, kx, ky, kz, c_wide, columns, count,
):
    core = core_ref[0]
    half = 0.5 * (1 - 2 * core).astype(jnp.float32)
    work[...] = jnp.zeros_like(work)
    visc[...] = jnp.zeros_like(visc)
    send[...] = jnp.zeros_like(send)
    for f in range(4):
        row = (lambda i, f=f: visc.at[i]) if f == 3 else (lambda i, f=f: work.at[f, i])
        row(0)[8:16] = near[256 + f * 8 : 264 + f * 8]
        for i in range(4):
            at = (f * 4 + i) * 16
            row(4 - i)[4:20] = near[at : at + 16]
        for x in range(2):
            at = f * 2 + x
            row(5 + x)[3:8] = low[at * 5 : at * 5 + 5]
            row(5 + x)[8:16] = fields[f, x]
            row(5 + x)[16:21] = high[at * 5 : at * 5 + 5]
            row(8 - x)[3:21] = mate[at * 18 : at * 18 + 18]
        for j in range(3):
            row(11 - j)[4:20] = mate_in[f, j]
    coefficients(visc, 12, kx, ky, kz)
    state = diffusion(work, spare, 0, 11, 0, kx, ky, kz)

    for c in range(3):
        for x in range(2):
            at = (c * 3) * 16 + x * 8
            own = state[c, 5 + x, 8:16]
            own_state[c, x] = own
            columns[at : at + 8] = half * (state[c, 6 + x, 8:16] - state[c, 4 + x, 8:16])
            columns[at + 16 : at + 24] = 0.5 * (state[c, 5 + x, 9:17] - state[c, 5 + x, 7:15])
            columns[at + 32 : at + 40] = 0.5 * (turned(own, -1, 1) - turned(own, 1, 1))
    for x in range(2):
        d = []
        for c in range(3):
            own = cot[c, x]
            c_wide[7:8] = low[40 + c * 2 + x : 41 + c * 2 + x]
            c_wide[8:16] = own
            c_wide[16:17] = high[40 + c * 2 + x : 41 + c * 2 + x]
            if x == 0:
                d_x = cot[c, 1] - edge[32 + c * 8 : 40 + c * 8]
            else:
                d_x = mate[176 + c * 8 : 184 + c * 8] - cot[c, 0]
            d_y = 0.5 * (c_wide[9:17] - c_wide[7:15])
            d_z = 0.5 * (turned(own, -1, 1) - turned(own, 1, 1))
            d.append((half * d_x, d_y, d_z))
        grads = (
            d[0][0], d[1][1], d[2][2],
            d[0][1] + d[1][0], d[0][2] + d[2][0], d[1][2] + d[2][1],
        )
        for k in range(6):
            columns[(9 + k) * 16 + x * 8 : (9 + k) * 16 + x * 8 + 8] = SCALE * grads[k]
    columns[240:256] = jnp.zeros((16, 128), jnp.float32)

    for e in range(count.shape[0]):
        count[e] = 0
    for k in range(16):
        owner = owner_ref[jnp.bitwise_xor(k, core * 8)]
        rank = count[owner]
        count[owner] = rank + 1
        slot = owner * CAP + rank
        slot_ref[k] = slot
        send[slot] = columns[pl.ds(k, 16, stride=16)]


def adjoint_kernel(core_ref, adjoint, visc, out, work, spare, kx, ky, kz):
    work[...] = jnp.zeros_like(work)
    for c in range(3):
        for i in range(10):
            work[c, i, 4:20] = adjoint[c, i]
    coefficients(visc, 12, kx, ky, kz)
    state = diffusion(work, spare, 0, 9, 1, kx, ky, kz)
    core = core_ref[0]
    for c in range(3):
        for x in range(2):
            out[c, jnp.bitwise_xor(x, core)] = state[c, 4 + x, 8:16]


def finish_kernel(whole, w_in, b_in, w_mid, b_mid, w_out, b_out):
    w_in[0] = whole[0:9]
    b_in[...] = whole[9:10]
    w_mid[0] = whole[10:138]
    b_mid[...] = whole[138:139]
    w_out[...] = whole[139:145]
    b_out[...] = whole[145:146]


def along_z(values):
    return 0.5 * (jnp.roll(values, -1, -1) - jnp.roll(values, 1, -1))


def step(velocity, viscosity, cotangent, assignment, w_in, b_in, w_mid, b_mid, w_out, b_out):
    experts = lax.axis_size("yz")
    core = lax.axis_index("gx") % 2
    sign = (1 - 2 * core).astype(jnp.float32)

    def mirror(v, dim):
        return jnp.where(core == 0, v, jnp.flip(v, dim))

    fields = jnp.concatenate([mirror(velocity, 1), mirror(viscosity, 0)[None]], axis=0)
    cot = mirror(cotangent, 1)
    core_arg = core.astype(jnp.int32).reshape(1)

    edge = across(packed([fields[:, 0], cot[:, 0]]))
    low, high = swap_y(
        packed([fields[:, :, 3:], cot[:, :, 7:]]), packed([fields[:, :, :5], cot[:, :, :1]])
    )
    f_low, f_high = low[:40].reshape(4, 2, 5, 128), high[:40].reshape(4, 2, 5, 128)
    wide = jnp.concatenate([f_low, fields, f_high], axis=2)
    mate = to_partner(packed([wide, edge[:32], cot[:, 1]]))
    partner = mate[:144].reshape(4, 2, 18, 128)
    chip = jnp.concatenate([wide, jnp.flip(partner, 1)], axis=1)
    near = across(packed([chip[:, :, 1:17], mate[144:176]]))
    pass_on = jnp.flip(near[:256].reshape(4, 4, 16, 128)[:, :3], 1)
    mate_in = to_partner(pass_on)
    f32, i32 = jnp.float32, jnp.int32
    wide_rows = [pltpu.VMEM((12, 24, 128), f32)] * 3
    send, own_state, visc, slot = call(
        forward_kernel,
        [
            ((experts * CAP, 16, 128), f32),
            ((3, 2, 8, 128), f32),
            ((12, 24, 128), f32),
            ((16,), i32),
        ],
        [pltpu.VMEM((3, 12, 24, 128), f32)] * 2
        + wide_rows
        + [pltpu.VMEM((24, 128), f32), pltpu.VMEM((256, 128), f32), pltpu.SMEM((experts,), i32)],
        (0, 1),
        (core_arg, assignment.reshape(16), fields, cot, low, high, edge, mate, near, mate_in),
        smem_outs=(3,),
    )
    recv = exchange(send.reshape(experts, CAP * 16, 128), "yz")
    recv = recv.reshape(experts * CAP, 16, 128)

    w1, w2, w3 = w_in[0], w_mid[0], w_out[0]
    turn = jnp.transpose(recv, (1, 0, 2)).reshape(16, -1)
    x = turn[:9]
    sg = turn[9:15]

    def dot(a, b, ca, cb):
        return lax.dot_general(a, b, (((ca,), (cb,)), ((), ())), precision=PREC)

    h1 = jnp.tanh(dot(w1, x, 0, 0) + b_in[0][:, None])
    h2 = jnp.tanh(dot(w2, h1, 0, 0) + b_mid[0][:, None])
    stress = dot(w3, h2, 0, 0) + b_out[0][:, None]
    g2 = dot(w3, sg, 1, 0) * (1.0 - h2 * h2)
    g1 = dot(w2, g2, 1, 0) * (1.0 - h1 * h1)
    fg = dot(w1, g1, 1, 0)
    grads = [
        dot(x, g1, 1, 1),
        jnp.sum(g1, axis=1)[None],
        dot(h1, g2, 1, 1),
        jnp.sum(g2, axis=1)[None],
        dot(sg, h2, 1, 1),
        jnp.pad(jnp.sum(sg, axis=1), (0, 122))[None],
    ]

    back = jnp.concatenate([fg, stress], axis=0).reshape(15, experts * CAP, 128)
    back = jnp.transpose(back, (1, 0, 2)).reshape(experts, CAP * 15, 128)
    home = exchange(back, "yz").reshape(experts * CAP, 15, 128)
    home = jnp.transpose(home[slot], (1, 0, 2)).reshape(15, 2, 8, 128)

    chips = lax.axis_size("gx") // 2
    vector = jnp.concatenate(grads, axis=0)
    chunk = -(-vector.shape[0] // chips)
    vector = vector + to_partner(vector)
    split = jnp.pad(vector, ((0, chunk * chips - vector.shape[0]), (0, 0))).reshape(chips, chunk, 128)
    groups = [list(range(0, 2 * chips, 2)), list(range(1, 2 * chips, 2))]
    parts = exchange(split, "gx", groups)
    mine = jnp.sum(parts, axis=0)
    whole = exchange(jnp.broadcast_to(mine, split.shape), "gx", groups).reshape(-1, 128)

    fgrad = home[:9].reshape(3, 3, 2, 8, 128)
    fx, fy, fz = fgrad[:, 0], fgrad[:, 1], fgrad[:, 2]
    tau = home[9:]
    tau_x = jnp.stack([tau[0], tau[3], tau[4]])
    tau_y = jnp.stack([tau[3], tau[1], tau[5]])
    tau_z = jnp.stack([tau[4], tau[5], tau[2]])
    part = cot - along_z(fz)
    low, high = swap_y(
        packed([part[:, :, 4:], fx[:, :, 4:], fy[:, :, 3:], tau_y[:, :, 7:]]),
        packed([part[:, :, :4], fx[:, :, :4], fy[:, :, :5], tau_y[:, :, :1]]),
    )
    rims = [(3, 2, 4, 128), (3, 2, 4, 128), (3, 2, 5, 128), (3, 2, 1, 128)]
    p_low, x_low, y_low, t_low = unpacked(low, rims)
    p_high, x_high, y_high, t_high = unpacked(high, rims)
    fy_wide = jnp.concatenate([y_low, fy, y_high], axis=2)
    part = jnp.concatenate([p_low, part, p_high], axis=2)
    part = part - 0.5 * (fy_wide[:, :, 2:] - fy_wide[:, :, :-2])
    fx_wide = jnp.concatenate([x_low, fx, x_high], axis=2)
    got = across(packed([fx[:, 0], tau_x[:, 0]]))
    fx_edge, tau_outer = unpacked(got, [(3, 8, 128), (3, 8, 128)])
    got = to_partner(packed([part, fx_wide, fx_edge, tau_x[:, 1]]))
    part_other, fx_other, fx_far, tau_other = unpacked(
        got, [part.shape, fx_wide.shape, (3, 8, 128), (3, 8, 128)]
    )
    part_chip = jnp.concatenate([part, jnp.flip(part_other, 1)], axis=1)
    fx_chip = jnp.concatenate([fx_wide, jnp.flip(fx_other, 1)], axis=1)
    half = 0.5 * sign
    zero = jnp.zeros_like(fx_chip[:, :1])
    fx_pad = jnp.concatenate([zero, fx_chip, zero], axis=1)
    adj_chip = part_chip - half * (fx_pad[:, 2:] - fx_pad[:, :-2])
    last = adj_chip[:, 3] - half * jnp.pad(fx_far, ((0, 0), (4, 4), (0, 0)))
    send = jnp.concatenate([adj_chip[:, :3], last[:, None]], axis=1)
    got = across(packed([send, fx_chip[:, 0]]))
    adj_outer, fx_outer = unpacked(got, [(3, 4, 16, 128), (3, 16, 128)])
    adj_outer = jnp.flip(adj_outer, 1)
    adj_outer = jnp.concatenate(
        [adj_outer[:, :3], adj_outer[:, 3:] - half * fx_chip[:, :1]], axis=1
    )
    got = to_partner(packed([adj_outer[:, 2:], fx_outer]))
    adj_inner, fx_inner = unpacked(got, [(3, 2, 16, 128), (3, 16, 128)])
    adjoint = jnp.concatenate(
        [
            adj_outer,
            adj_chip[:, :1] + half * fx_outer[:, None],
            adj_chip[:, 1:3],
            adj_chip[:, 3:] - half * fx_inner[:, None],
            jnp.flip(adj_inner, 1),
        ],
        axis=1,
    )
    (grad_velocity,) = call(
        adjoint_kernel,
        [((3, 2, 8, 128), f32)],
        [pltpu.VMEM((3, 10, 24, 128), f32)] * 2 + wide_rows,
        (0,),
        (core_arg, adjoint, visc),
    )

    t_x = jnp.concatenate([tau_outer[:, None], tau_x, tau_other[:, None]], axis=1)
    t_y = jnp.concatenate([t_low, tau_y, t_high], axis=2)
    predicted = own_state - SCALE * (
        half * (t_x[:, 2:] - t_x[:, :2]) + 0.5 * (t_y[:, :, 2:] - t_y[:, :, :-2]) + along_z(tau_z)
    )
    results = call(
        finish_kernel,
        [
            ((1, 9, 128), f32),
            ((1, 128), f32),
            ((1, 128, 128), f32),
            ((1, 128), f32),
            ((6, 128), f32),
            ((1, 128), f32),
        ],
        [],
        (),
        (whole,),
    )
    g_w_in, g_b_in, g_w_mid, g_b_mid, g_w_out, g_b_out = results
    return (
        mirror(predicted, 1),
        grad_velocity,
        g_w_in,
        g_b_in,
        g_w_mid,
        g_b_mid,
        jnp.transpose(g_w_out)[None],
        g_b_out[:, :6],
    )


def solution(mesh):
    placed = (
        P(None, "gx", "yz", None),
        P("gx", "yz", None),
        P(None, "gx", "yz", None),
        P(("gx", "yz"), None),
        P("yz", None, None),
        P("yz", None),
        P("yz", None, None),
        P("yz", None),
        P("yz", None, None),
        P("yz", None),
    )
    return jax.shard_map(
        step,
        mesh=mesh,
        in_specs=placed,
        out_specs=(
            P(None, "gx", "yz", None),
            P(None, "gx", "yz", None),
            P("yz", None, None),
            P("yz", None),
            P("yz", None, None),
            P("yz", None),
            P("yz", None, None),
            P("yz", None),
        ),
        check_vma=False,
    )
```

```python
import jax
import jax.numpy as jnp
from jax import lax
from jax.experimental import pallas as pl
from jax.experimental.pallas import tpu as pltpu
from jax.sharding import PartitionSpec as P

SUBSTEPS = 4
STEP = 0.15
SCALE = 0.5
CAP = 2
PREC = lax.Precision.HIGH
AXES = ("gx", "yz")
INTERPRET = False


def permute(value, target):
    n_gx, n_yz = lax.axis_size("gx"), lax.axis_size("yz")
    pairs = []
    for g in range(n_gx):
        for y in range(n_yz):
            to_g, to_y = target(g, y)
            pairs.append((g * n_yz + y, (to_g % n_gx) * n_yz + to_y % n_yz))
    return lax.ppermute(value, AXES, pairs)


def exchange(value, axis, groups=None):
    return lax.all_to_all(value, axis, 0, 0, axis_index_groups=groups, tiled=True)


def to_partner(value):
    return permute(value, lambda g, y: (g ^ 1, y))


def across(value):
    return permute(value, lambda g, y: (g - 1 if g % 2 == 0 else g + 1, y))


def packed(pieces):
    return jnp.concatenate([p.reshape(-1, 128) for p in pieces], axis=0)


def unpacked(buffer, shapes):
    pieces, at = [], 0
    for shape in shapes:
        rows = 1
        for n in shape[:-1]:
            rows *= n
        pieces.append(buffer[at : at + rows].reshape(shape))
        at += rows
    return pieces


def swap_y(low, high):
    below = permute(low, lambda g, y: (g, y + 1))
    above = permute(high, lambda g, y: (g, y - 1))
    return below, above


def spec(space):
    return pl.BlockSpec(memory_space=space)


def call(kernel, outs, scratch, smem_ins, args, smem_outs=(), vmem_outs=()):
    if not INTERPRET:
        args = [
            arg if i in smem_ins else pltpu.with_memory_space_constraint(arg, pltpu.VMEM)
            for i, arg in enumerate(args)
        ]
    vmem_outs = () if INTERPRET else vmem_outs
    return pl.pallas_call(
        kernel,
        out_shape=[
            (pltpu.VMEM if i in vmem_outs else jax.ShapeDtypeStruct)(shape, dtype)
            for i, (shape, dtype) in enumerate(outs)
        ],
        in_specs=[spec(pltpu.SMEM if i in smem_ins else pltpu.VMEM) for i in range(len(args))],
        out_specs=[spec(pltpu.SMEM if i in smem_outs else pltpu.VMEM) for i in range(len(outs))],
        scratch_shapes=scratch,
        interpret=INTERPRET,
    )(*args)


def turned(value, shift, axis):
    return pltpu.roll(value, shift % value.shape[axis], axis)


def coefficients(visc, rows, kx, ky, kz):
    for i in range(rows):
        own = visc[i]
        ky[i] = 0.5 * (own + turned(own, -1, 0))
        kz[i] = 0.5 * (own + turned(own, -1, 1))
        if i + 1 < rows:
            kx[i] = 0.5 * (own + visc[i + 1])


def diffusion(state, other, first, last, k_at, kx, ky, kz):
    for _ in range(SUBSTEPS):
        first, last = first + 1, last - 1
        for c in range(3):
            center = state[c, first]
            below = kx[k_at + first - 1] * (center - state[c, first - 1])
            for i in range(first, last + 1):
                k = k_at + i
                upper = state[c, i + 1]
                above = kx[k] * (upper - center)
                y_flux = ky[k] * (turned(center, -1, 0) - center)
                z_flux = kz[k] * (turned(center, -1, 1) - center)
                total = (above - below) + (y_flux - turned(y_flux, 1, 0))
                total = total + (z_flux - turned(z_flux, 1, 1))
                other[c, i] = center + STEP * total
                below, center = above, upper
        state, other = other, state
    return state


def forward_kernel(
    core_ref, owner_ref, fields, cot, low, high, edge, mate, near, mate_in,
    send, own_state, visc, slot_ref,
    work, spare, kx, ky, kz, c_wide, columns, count,
):
    core = core_ref[0]
    half = 0.5 * (1 - 2 * core).astype(jnp.float32)
    work[...] = jnp.zeros_like(work)
    visc[...] = jnp.zeros_like(visc)
    send[...] = jnp.zeros_like(send)
    for f in range(4):
        row = (lambda i, f=f: visc.at[i]) if f == 3 else (lambda i, f=f: work.at[f, i])
        row(0)[8:16] = near[256 + f * 8 : 264 + f * 8]
        for i in range(4):
            at = (f * 4 + i) * 16
            row(4 - i)[4:20] = near[at : at + 16]
        for x in range(2):
            at = f * 2 + x
            row(5 + x)[3:8] = low[at * 5 : at * 5 + 5]
            row(5 + x)[8:16] = fields[f, x]
            row(5 + x)[16:21] = high[at * 5 : at * 5 + 5]
            row(8 - x)[3:21] = mate[at * 18 : at * 18 + 18]
        for j in range(3):
            row(11 - j)[4:20] = mate_in[f, j]
    coefficients(visc, 12, kx, ky, kz)
    state = diffusion(work, spare, 0, 11, 0, kx, ky, kz)

    for c in range(3):
        for x in range(2):
            at = (c * 3) * 16 + x * 8
            own = state[c, 5 + x, 8:16]
            own_state[c, x] = own
            columns[at : at + 8] = half * (state[c, 6 + x, 8:16] - state[c, 4 + x, 8:16])
            columns[at + 16 : at + 24] = 0.5 * (state[c, 5 + x, 9:17] - state[c, 5 + x, 7:15])
            columns[at + 32 : at + 40] = 0.5 * (turned(own, -1, 1) - turned(own, 1, 1))
    for x in range(2):
        d = []
        for c in range(3):
            own = cot[c, x]
            c_wide[7:8] = low[40 + c * 2 + x : 41 + c * 2 + x]
            c_wide[8:16] = own
            c_wide[16:17] = high[40 + c * 2 + x : 41 + c * 2 + x]
            if x == 0:
                d_x = cot[c, 1] - edge[32 + c * 8 : 40 + c * 8]
            else:
                d_x = mate[176 + c * 8 : 184 + c * 8] - cot[c, 0]
            d_y = 0.5 * (c_wide[9:17] - c_wide[7:15])
            d_z = 0.5 * (turned(own, -1, 1) - turned(own, 1, 1))
            d.append((half * d_x, d_y, d_z))
        grads = (
            d[0][0], d[1][1], d[2][2],
            d[0][1] + d[1][0], d[0][2] + d[2][0], d[1][2] + d[2][1],
        )
        for k in range(6):
            columns[(9 + k) * 16 + x * 8 : (9 + k) * 16 + x * 8 + 8] = SCALE * grads[k]
    columns[240:256] = jnp.zeros((16, 128), jnp.float32)

    for e in range(count.shape[0]):
        count[e] = 0
    for k in range(16):
        owner = owner_ref[jnp.bitwise_xor(k, core * 8)]
        rank = count[owner]
        count[owner] = rank + 1
        slot = owner * CAP + rank
        slot_ref[k] = slot
        send[slot] = columns[pl.ds(k, 16, stride=16)]


def adjoint_kernel(core_ref, adjoint, visc, out, work, spare, kx, ky, kz):
    work[...] = jnp.zeros_like(work)
    for c in range(3):
        for i in range(10):
            work[c, i, 4:20] = adjoint[c, i]
    coefficients(visc, 12, kx, ky, kz)
    state = diffusion(work, spare, 0, 9, 1, kx, ky, kz)
    core = core_ref[0]
    for c in range(3):
        for x in range(2):
            out[c, jnp.bitwise_xor(x, core)] = state[c, 4 + x, 8:16]


def finish_kernel(whole, w_in, b_in, w_mid, b_mid, w_out, b_out):
    for i in range(9):
        w_in[i] = whole[i : i + 1]
    for i in range(6):
        w_out[i] = whole[139 + i : 140 + i]
    b_in[...] = whole[9:10]
    w_mid[0] = whole[10:138]
    b_mid[...] = whole[138:139]
    b_out[...] = whole[145:146]


def along_z(values):
    return 0.5 * (jnp.roll(values, -1, -1) - jnp.roll(values, 1, -1))


def step(velocity, viscosity, cotangent, assignment, w_in, b_in, w_mid, b_mid, w_out, b_out):
    experts = lax.axis_size("yz")
    core = lax.axis_index("gx") % 2
    sign = (1 - 2 * core).astype(jnp.float32)

    def mirror(v, dim):
        return jnp.where(core == 0, v, jnp.flip(v, dim))

    fields = jnp.concatenate([mirror(velocity, 1), mirror(viscosity, 0)[None]], axis=0)
    cot = mirror(cotangent, 1)
    core_arg = core.astype(jnp.int32).reshape(1)

    edge = across(packed([fields[:, 0], cot[:, 0]]))
    low, high = swap_y(
        packed([fields[:, :, 3:], cot[:, :, 7:]]), packed([fields[:, :, :5], cot[:, :, :1]])
    )
    f_low, f_high = low[:40].reshape(4, 2, 5, 128), high[:40].reshape(4, 2, 5, 128)
    wide = jnp.concatenate([f_low, fields, f_high], axis=2)
    mate = to_partner(packed([wide, edge[:32], cot[:, 1]]))
    partner = mate[:144].reshape(4, 2, 18, 128)
    chip = jnp.concatenate([wide, jnp.flip(partner, 1)], axis=1)
    near = across(packed([chip[:, :, 1:17], mate[144:176]]))
    pass_on = jnp.flip(near[:256].reshape(4, 4, 16, 128)[:, :3], 1)
    mate_in = to_partner(pass_on)
    f32, i32 = jnp.float32, jnp.int32
    wide_rows = [pltpu.VMEM((12, 24, 128), f32)] * 3
    send, own_state, visc, slot = call(
        forward_kernel,
        [
            ((experts * CAP, 16, 128), f32),
            ((3, 2, 8, 128), f32),
            ((12, 24, 128), f32),
            ((16,), i32),
        ],
        [pltpu.VMEM((3, 12, 24, 128), f32)] * 2
        + wide_rows
        + [pltpu.VMEM((24, 128), f32), pltpu.VMEM((256, 128), f32), pltpu.SMEM((experts,), i32)],
        (0, 1),
        (core_arg, assignment.reshape(16), fields, cot, low, high, edge, mate, near, mate_in),
        smem_outs=(3,),
        vmem_outs=(1, 2),
    )
    recv = exchange(send.reshape(experts, CAP * 16, 128), "yz")
    recv = recv.reshape(experts * CAP, 16, 128)

    w1, w2, w3 = w_in[0], w_mid[0], w_out[0]
    turn = jnp.transpose(recv, (1, 0, 2)).reshape(16, -1)
    x = turn[:9]
    sg = turn[9:15]

    def dot(a, b, ca, cb):
        return lax.dot_general(a, b, (((ca,), (cb,)), ((), ())), precision=PREC)

    h1 = jnp.tanh(dot(w1, x, 0, 0) + b_in[0][:, None])
    h2 = jnp.tanh(dot(w2, h1, 0, 0) + b_mid[0][:, None])
    stress = dot(w3, h2, 0, 0) + b_out[0][:, None]
    g2 = dot(w3, sg, 1, 0) * (1.0 - h2 * h2)
    g1 = dot(w2, g2, 1, 0) * (1.0 - h1 * h1)
    fg = dot(w1, g1, 1, 0)
    grads = [
        dot(x, g1, 1, 1),
        jnp.sum(g1, axis=1)[None],
        dot(h1, g2, 1, 1),
        jnp.sum(g2, axis=1)[None],
        dot(sg, h2, 1, 1),
        jnp.pad(jnp.sum(sg, axis=1), (0, 122))[None],
    ]

    back = jnp.concatenate([fg, stress], axis=0).reshape(15, experts * CAP, 128)
    back = jnp.transpose(back, (1, 0, 2)).reshape(experts, CAP * 15, 128)
    home = exchange(back, "yz").reshape(experts * CAP, 15, 128)
    home = jnp.transpose(home[slot], (1, 0, 2)).reshape(15, 2, 8, 128)

    chips = lax.axis_size("gx") // 2
    vector = jnp.concatenate(grads, axis=0)
    chunk = -(-vector.shape[0] // chips)
    vector = vector + to_partner(vector)
    split = jnp.pad(vector, ((0, chunk * chips - vector.shape[0]), (0, 0))).reshape(chips, chunk, 128)
    groups = [list(range(0, 2 * chips, 2)), list(range(1, 2 * chips, 2))]
    parts = exchange(split, "gx", groups)
    mine = jnp.sum(parts, axis=0)
    whole = exchange(jnp.broadcast_to(mine, split.shape), "gx", groups).reshape(-1, 128)

    fgrad = home[:9].reshape(3, 3, 2, 8, 128)
    fx, fy, fz = fgrad[:, 0], fgrad[:, 1], fgrad[:, 2]
    tau = home[9:]
    tau_x = jnp.stack([tau[0], tau[3], tau[4]])
    tau_y = jnp.stack([tau[3], tau[1], tau[5]])
    tau_z = jnp.stack([tau[4], tau[5], tau[2]])
    part = cot - along_z(fz)
    low, high = swap_y(
        packed([part[:, :, 4:], fx[:, :, 4:], fy[:, :, 3:], tau_y[:, :, 7:]]),
        packed([part[:, :, :4], fx[:, :, :4], fy[:, :, :5], tau_y[:, :, :1]]),
    )
    rims = [(3, 2, 4, 128), (3, 2, 4, 128), (3, 2, 5, 128), (3, 2, 1, 128)]
    p_low, x_low, y_low, t_low = unpacked(low, rims)
    p_high, x_high, y_high, t_high = unpacked(high, rims)
    fy_wide = jnp.concatenate([y_low, fy, y_high], axis=2)
    part = jnp.concatenate([p_low, part, p_high], axis=2)
    part = part - 0.5 * (fy_wide[:, :, 2:] - fy_wide[:, :, :-2])
    fx_wide = jnp.concatenate([x_low, fx, x_high], axis=2)
    got = across(packed([fx[:, 0], tau_x[:, 0]]))
    fx_edge, tau_outer = unpacked(got, [(3, 8, 128), (3, 8, 128)])
    got = to_partner(packed([part, fx_wide, fx_edge, tau_x[:, 1]]))
    part_other, fx_other, fx_far, tau_other = unpacked(
        got, [part.shape, fx_wide.shape, (3, 8, 128), (3, 8, 128)]
    )
    part_chip = jnp.concatenate([part, jnp.flip(part_other, 1)], axis=1)
    fx_chip = jnp.concatenate([fx_wide, jnp.flip(fx_other, 1)], axis=1)
    half = 0.5 * sign
    zero = jnp.zeros_like(fx_chip[:, :1])
    fx_pad = jnp.concatenate([zero, fx_chip, zero], axis=1)
    adj_chip = part_chip - half * (fx_pad[:, 2:] - fx_pad[:, :-2])
    last = adj_chip[:, 3] - half * jnp.pad(fx_far, ((0, 0), (4, 4), (0, 0)))
    send = jnp.concatenate([adj_chip[:, :3], last[:, None]], axis=1)
    got = across(packed([send, fx_chip[:, 0]]))
    adj_outer, fx_outer = unpacked(got, [(3, 4, 16, 128), (3, 16, 128)])
    adj_outer = jnp.flip(adj_outer, 1)
    adj_outer = jnp.concatenate(
        [adj_outer[:, :3], adj_outer[:, 3:] - half * fx_chip[:, :1]], axis=1
    )
    got = to_partner(packed([adj_outer[:, 2:], fx_outer]))
    adj_inner, fx_inner = unpacked(got, [(3, 2, 16, 128), (3, 16, 128)])
    adjoint = jnp.concatenate(
        [
            adj_outer,
            adj_chip[:, :1] + half * fx_outer[:, None],
            adj_chip[:, 1:3],
            adj_chip[:, 3:] - half * fx_inner[:, None],
            jnp.flip(adj_inner, 1),
        ],
        axis=1,
    )
    (grad_velocity,) = call(
        adjoint_kernel,
        [((3, 2, 8, 128), f32)],
        [pltpu.VMEM((3, 10, 24, 128), f32)] * 2 + wide_rows,
        (0,),
        (core_arg, adjoint, visc),
    )

    t_x = jnp.concatenate([tau_outer[:, None], tau_x, tau_other[:, None]], axis=1)
    t_y = jnp.concatenate([t_low, tau_y, t_high], axis=2)
    predicted = own_state - SCALE * (
        half * (t_x[:, 2:] - t_x[:, :2]) + 0.5 * (t_y[:, :, 2:] - t_y[:, :, :-2]) + along_z(tau_z)
    )
    results = call(
        finish_kernel,
        [
            ((9, 1, 128), f32),
            ((1, 128), f32),
            ((1, 128, 128), f32),
            ((1, 128), f32),
            ((6, 1, 128), f32),
            ((1, 128), f32),
        ],
        [],
        (),
        (whole,),
    )
    g_w_in, g_b_in, g_w_mid, g_b_mid, g_w_out, g_b_out = results
    return (
        mirror(predicted, 1),
        grad_velocity,
        jnp.transpose(g_w_in, (1, 0, 2)),
        g_b_in,
        g_w_mid,
        g_b_mid,
        jnp.transpose(g_w_out, (1, 2, 0)),
        g_b_out[:, :6],
    )


def solution(mesh):
    placed = (
        P(None, "gx", "yz", None),
        P("gx", "yz", None),
        P(None, "gx", "yz", None),
        P(("gx", "yz"), None),
        P("yz", None, None),
        P("yz", None),
        P("yz", None, None),
        P("yz", None),
        P("yz", None, None),
        P("yz", None),
    )
    return jax.shard_map(
        step,
        mesh=mesh,
        in_specs=placed,
        out_specs=(
            P(None, "gx", "yz", None),
            P(None, "gx", "yz", None),
            P("yz", None, None),
            P("yz", None),
            P("yz", None, None),
            P("yz", None),
            P("yz", None, None),
            P("yz", None),
        ),
        check_vma=False,
    )
```

```python
import jax
import jax.numpy as jnp
from jax import lax
from jax.experimental import pallas as pl
from jax.experimental.pallas import tpu as pltpu
from jax.sharding import PartitionSpec as P

SUBSTEPS = 4
STEP = 0.15
SCALE = 0.5
CAP = 2
PREC = lax.Precision.HIGH
AXES = ("gx", "yz")
INTERPRET = False
NEAR_WIDTH = (16, 14, 12, 10, 8)
NEAR_AT = (0, 64, 120, 168, 208)


def permute(value, target):
    n_gx, n_yz = lax.axis_size("gx"), lax.axis_size("yz")
    pairs = []
    for g in range(n_gx):
        for y in range(n_yz):
            to_g, to_y = target(g, y)
            pairs.append((g * n_yz + y, (to_g % n_gx) * n_yz + to_y % n_yz))
    return lax.ppermute(value, AXES, pairs)


def exchange(value, axis, groups=None):
    return lax.all_to_all(value, axis, 0, 0, axis_index_groups=groups, tiled=True)


def to_partner(value):
    return permute(value, lambda g, y: (g ^ 1, y))


def across(value):
    return permute(value, lambda g, y: (g - 1 if g % 2 == 0 else g + 1, y))


def packed(pieces):
    return jnp.concatenate([p.reshape(-1, 128) for p in pieces], axis=0)


def unpacked(buffer, shapes):
    pieces, at = [], 0
    for shape in shapes:
        rows = 1
        for n in shape[:-1]:
            rows *= n
        pieces.append(buffer[at : at + rows].reshape(shape))
        at += rows
    return pieces


def swap_y(low, high):
    below = permute(low, lambda g, y: (g, y + 1))
    above = permute(high, lambda g, y: (g, y - 1))
    return below, above


def spec(space):
    return pl.BlockSpec(memory_space=space)


def call(kernel, outs, scratch, smem_ins, args, smem_outs=(), vmem_outs=()):
    if not INTERPRET:
        args = [
            arg if i in smem_ins else pltpu.with_memory_space_constraint(arg, pltpu.VMEM)
            for i, arg in enumerate(args)
        ]
    vmem_outs = () if INTERPRET else vmem_outs
    return pl.pallas_call(
        kernel,
        out_shape=[
            (pltpu.VMEM if i in vmem_outs else jax.ShapeDtypeStruct)(shape, dtype)
            for i, (shape, dtype) in enumerate(outs)
        ],
        in_specs=[spec(pltpu.SMEM if i in smem_ins else pltpu.VMEM) for i in range(len(args))],
        out_specs=[spec(pltpu.SMEM if i in smem_outs else pltpu.VMEM) for i in range(len(outs))],
        scratch_shapes=scratch,
        interpret=INTERPRET,
    )(*args)


def turned(value, shift, axis):
    return pltpu.roll(value, shift % value.shape[axis], axis)


def coefficients(visc, rows, kx, ky, kz):
    for i in range(rows):
        own = visc[i]
        ky[i] = 0.5 * (own + turned(own, -1, 0))
        kz[i] = 0.5 * (own + turned(own, -1, 1))
        if i + 1 < rows:
            kx[i] = 0.5 * (own + visc[i + 1])


def diffusion(state, other, first, last, k_at, kx, ky, kz):
    for _ in range(SUBSTEPS):
        first, last = first + 1, last - 1
        for c in range(3):
            center = state[c, first]
            below = kx[k_at + first - 1] * (center - state[c, first - 1])
            for i in range(first, last + 1):
                k = k_at + i
                upper = state[c, i + 1]
                above = kx[k] * (upper - center)
                y_flux = ky[k] * (turned(center, -1, 0) - center)
                z_flux = kz[k] * (turned(center, -1, 1) - center)
                total = (above - below) + (y_flux - turned(y_flux, 1, 0))
                total = total + (z_flux - turned(z_flux, 1, 1))
                other[c, i] = center + STEP * total
                below, center = above, upper
        state, other = other, state
    return state


def placed(core, owner_ref, slot_ref, count):
    for e in range(count.shape[0]):
        count[e] = 0
    for k in range(16):
        owner = owner_ref[jnp.bitwise_xor(k, core * 8)]
        rank = count[owner]
        count[owner] = rank + 1
        slot_ref[k] = owner * CAP + rank


def stress_kernel(
    core_ref, owner_ref, cot, low, high, edge, mate, send, slot_ref, c_wide, columns, count
):
    core = core_ref[0]
    half = 0.5 * (1 - 2 * core).astype(jnp.float32)
    send[...] = jnp.zeros_like(send)
    placed(core, owner_ref, slot_ref, count)
    for x in range(2):
        d = []
        for c in range(3):
            own = cot[c, x]
            c_wide[7:8] = low[40 + c * 2 + x : 41 + c * 2 + x]
            c_wide[8:16] = own
            c_wide[16:17] = high[40 + c * 2 + x : 41 + c * 2 + x]
            if x == 0:
                d_x = cot[c, 1] - edge[32 + c * 8 : 40 + c * 8]
            else:
                d_x = mate[176 + c * 8 : 184 + c * 8] - cot[c, 0]
            d_y = 0.5 * (c_wide[9:17] - c_wide[7:15])
            d_z = 0.5 * (turned(own, -1, 1) - turned(own, 1, 1))
            d.append((half * d_x, d_y, d_z))
        grads = (
            d[0][0], d[1][1], d[2][2],
            d[0][1] + d[1][0], d[0][2] + d[2][0], d[1][2] + d[2][1],
        )
        for k in range(6):
            columns[k * 16 + x * 8 : k * 16 + x * 8 + 8] = SCALE * grads[k]
    for k in range(16):
        send[slot_ref[k]] = columns[pl.ds(k, 6, stride=16)]


def forward_kernel(
    core_ref, slot_ref, fields, low, high, mate, near, mate_in,
    send, own_state, visc,
    work, spare, kx, ky, kz, columns,
):
    half = 0.5 * (1 - 2 * core_ref[0]).astype(jnp.float32)
    work[...] = jnp.zeros_like(work)
    visc[...] = jnp.zeros_like(visc)
    send[...] = jnp.zeros_like(send)
    for f in range(4):
        row = (lambda i, f=f: visc.at[i]) if f == 3 else (lambda i, f=f: work.at[f, i])
        for j in range(5):
            at = NEAR_AT[j] + f * NEAR_WIDTH[j]
            row(4 - j)[4 + j : 20 - j] = near[at : at + NEAR_WIDTH[j]]
            if j < 3:
                row(9 + j)[4 + j : 20 - j] = mate_in[at : at + NEAR_WIDTH[j]]
        for x in range(2):
            at = f * 2 + x
            row(5 + x)[3:8] = low[at * 5 : at * 5 + 5]
            row(5 + x)[8:16] = fields[f, x]
            row(5 + x)[16:21] = high[at * 5 : at * 5 + 5]
            row(8 - x)[3:21] = mate[at * 18 : at * 18 + 18]
    coefficients(visc, 12, kx, ky, kz)
    state = diffusion(work, spare, 0, 11, 0, kx, ky, kz)

    for c in range(3):
        for x in range(2):
            at = (c * 3) * 16 + x * 8
            own = state[c, 5 + x, 8:16]
            own_state[c, x] = own
            columns[at : at + 8] = half * (state[c, 6 + x, 8:16] - state[c, 4 + x, 8:16])
            columns[at + 16 : at + 24] = 0.5 * (state[c, 5 + x, 9:17] - state[c, 5 + x, 7:15])
            columns[at + 32 : at + 40] = 0.5 * (turned(own, -1, 1) - turned(own, 1, 1))
    for k in range(16):
        send[slot_ref[k]] = columns[pl.ds(k, 9, stride=16)]


def adjoint_kernel(core_ref, adjoint, visc, out, work, spare, kx, ky, kz):
    work[...] = jnp.zeros_like(work)
    for c in range(3):
        for i in range(10):
            work[c, i, 4:20] = adjoint[c, i]
    coefficients(visc, 12, kx, ky, kz)
    state = diffusion(work, spare, 0, 9, 1, kx, ky, kz)
    core = core_ref[0]
    for c in range(3):
        for x in range(2):
            out[c, jnp.bitwise_xor(x, core)] = state[c, 4 + x, 8:16]


def finish_kernel(whole, w_in, b_in, w_mid, b_mid, w_out, b_out):
    for i in range(9):
        w_in[i] = whole[i : i + 1]
    for i in range(6):
        w_out[i] = whole[139 + i : 140 + i]
    b_in[...] = whole[9:10]
    w_mid[0] = whole[10:138]
    b_mid[...] = whole[138:139]
    b_out[...] = whole[145:146]


def along_z(values):
    return 0.5 * (jnp.roll(values, -1, -1) - jnp.roll(values, 1, -1))


def step(velocity, viscosity, cotangent, assignment, w_in, b_in, w_mid, b_mid, w_out, b_out):
    experts = lax.axis_size("yz")
    core = lax.axis_index("gx") % 2
    sign = (1 - 2 * core).astype(jnp.float32)

    def mirror(v, dim):
        return jnp.where(core == 0, v, jnp.flip(v, dim))

    fields = jnp.concatenate([mirror(velocity, 1), mirror(viscosity, 0)[None]], axis=0)
    cot = mirror(cotangent, 1)
    core_arg = core.astype(jnp.int32).reshape(1)

    edge = across(packed([fields[:, 0], cot[:, 0]]))
    low, high = swap_y(
        packed([fields[:, :, 3:], cot[:, :, 7:]]), packed([fields[:, :, :5], cot[:, :, :1]])
    )
    f_low, f_high = low[:40].reshape(4, 2, 5, 128), high[:40].reshape(4, 2, 5, 128)
    wide = jnp.concatenate([f_low, fields, f_high], axis=2)
    mate = to_partner(packed([wide, edge[:32], cot[:, 1]]))
    partner = mate[:144].reshape(4, 2, 18, 128)
    chip = jnp.concatenate([wide, jnp.flip(partner, 1)], axis=1)
    reach = [chip[:, j, 1 + j : 17 - j] for j in range(4)]
    near = across(packed(reach + [mate[144:176]]))
    mate_in = to_partner(near[:168])
    f32, i32 = jnp.float32, jnp.int32
    send_grad, slot = call(
        stress_kernel,
        [((experts * CAP, 6, 128), f32), ((16,), i32)],
        [pltpu.VMEM((24, 128), f32), pltpu.VMEM((128, 128), f32), pltpu.SMEM((experts,), i32)],
        (0, 1),
        (core_arg, assignment.reshape(16), cot, low, high, edge, mate),
        smem_outs=(1,),
    )
    got_grad = exchange(send_grad.reshape(experts, CAP * 6, 128), "yz")
    wide_rows = [pltpu.VMEM((12, 24, 128), f32)] * 3
    send, own_state, visc = call(
        forward_kernel,
        [((experts * CAP, 9, 128), f32), ((3, 2, 8, 128), f32), ((12, 24, 128), f32)],
        [pltpu.VMEM((3, 12, 24, 128), f32)] * 2 + wide_rows + [pltpu.VMEM((256, 128), f32)],
        (0, 1),
        (core_arg, slot, fields, low, high, mate, near, mate_in),
        vmem_outs=(1, 2),
    )
    recv = exchange(send.reshape(experts, CAP * 9, 128), "yz")
    x = jnp.transpose(recv.reshape(experts * CAP, 9, 128), (1, 0, 2)).reshape(9, -1)
    sg = jnp.transpose(got_grad.reshape(experts * CAP, 6, 128), (1, 0, 2)).reshape(6, -1)

    w1, w2, w3 = w_in[0], w_mid[0], w_out[0]

    def dot(a, b, ca, cb):
        return lax.dot_general(a, b, (((ca,), (cb,)), ((), ())), precision=PREC)

    h1 = jnp.tanh(dot(w1, x, 0, 0) + b_in[0][:, None])
    h2 = jnp.tanh(dot(w2, h1, 0, 0) + b_mid[0][:, None])
    stress = dot(w3, h2, 0, 0) + b_out[0][:, None]
    g2 = dot(w3, sg, 1, 0) * (1.0 - h2 * h2)
    g1 = dot(w2, g2, 1, 0) * (1.0 - h1 * h1)
    fg = dot(w1, g1, 1, 0)
    grads = [
        dot(x, g1, 1, 1),
        jnp.sum(g1, axis=1)[None],
        dot(h1, g2, 1, 1),
        jnp.sum(g2, axis=1)[None],
        dot(sg, h2, 1, 1),
        jnp.pad(jnp.sum(sg, axis=1), (0, 122))[None],
    ]

    back = jnp.concatenate([fg, stress], axis=0).reshape(15, experts * CAP, 128)
    back = jnp.transpose(back, (1, 0, 2)).reshape(experts, CAP * 15, 128)
    home = exchange(back, "yz").reshape(experts * CAP, 15, 128)
    home = jnp.transpose(home[slot], (1, 0, 2)).reshape(15, 2, 8, 128)

    chips = lax.axis_size("gx") // 2
    vector = jnp.concatenate(grads, axis=0)
    chunk = -(-vector.shape[0] // chips)
    vector = vector + to_partner(vector)
    split = jnp.pad(vector, ((0, chunk * chips - vector.shape[0]), (0, 0))).reshape(chips, chunk, 128)
    groups = [list(range(0, 2 * chips, 2)), list(range(1, 2 * chips, 2))]
    parts = exchange(split, "gx", groups)
    mine = jnp.sum(parts, axis=0)
    whole = exchange(jnp.broadcast_to(mine, split.shape), "gx", groups).reshape(-1, 128)

    fgrad = home[:9].reshape(3, 3, 2, 8, 128)
    fx, fy, fz = fgrad[:, 0], fgrad[:, 1], fgrad[:, 2]
    tau = home[9:]
    tau_x = jnp.stack([tau[0], tau[3], tau[4]])
    tau_y = jnp.stack([tau[3], tau[1], tau[5]])
    tau_z = jnp.stack([tau[4], tau[5], tau[2]])
    part = cot - along_z(fz)
    low, high = swap_y(
        packed([part[:, :, 4:], fx[:, :, 4:], fy[:, :, 3:], tau_y[:, :, 7:]]),
        packed([part[:, :, :4], fx[:, :, :4], fy[:, :, :5], tau_y[:, :, :1]]),
    )
    rims = [(3, 2, 4, 128), (3, 2, 4, 128), (3, 2, 5, 128), (3, 2, 1, 128)]
    p_low, x_low, y_low, t_low = unpacked(low, rims)
    p_high, x_high, y_high, t_high = unpacked(high, rims)
    fy_wide = jnp.concatenate([y_low, fy, y_high], axis=2)
    part = jnp.concatenate([p_low, part, p_high], axis=2)
    part = part - 0.5 * (fy_wide[:, :, 2:] - fy_wide[:, :, :-2])
    fx_wide = jnp.concatenate([x_low, fx, x_high], axis=2)
    got = across(packed([fx[:, 0], tau_x[:, 0]]))
    fx_edge, tau_outer = unpacked(got, [(3, 8, 128), (3, 8, 128)])
    got = to_partner(packed([part, fx_wide, fx_edge, tau_x[:, 1]]))
    part_other, fx_other, fx_far, tau_other = unpacked(
        got, [part.shape, fx_wide.shape, (3, 8, 128), (3, 8, 128)]
    )
    part_chip = jnp.concatenate([part, jnp.flip(part_other, 1)], axis=1)
    fx_chip = jnp.concatenate([fx_wide, jnp.flip(fx_other, 1)], axis=1)
    half = 0.5 * sign
    zero = jnp.zeros_like(fx_chip[:, :1])
    fx_pad = jnp.concatenate([zero, fx_chip, zero], axis=1)
    adj_chip = part_chip - half * (fx_pad[:, 2:] - fx_pad[:, :-2])
    last = adj_chip[:, 3] - half * jnp.pad(fx_far, ((0, 0), (4, 4), (0, 0)))
    send = jnp.concatenate([adj_chip[:, :3], last[:, None]], axis=1)
    got = across(packed([send, fx_chip[:, 0]]))
    adj_outer, fx_outer = unpacked(got, [(3, 4, 16, 128), (3, 16, 128)])
    adj_outer = jnp.flip(adj_outer, 1)
    adj_outer = jnp.concatenate(
        [adj_outer[:, :3], adj_outer[:, 3:] - half * fx_chip[:, :1]], axis=1
    )
    got = to_partner(packed([adj_outer[:, 2:], fx_outer]))
    adj_inner, fx_inner = unpacked(got, [(3, 2, 16, 128), (3, 16, 128)])
    adjoint = jnp.concatenate(
        [
            adj_outer,
            adj_chip[:, :1] + half * fx_outer[:, None],
            adj_chip[:, 1:3],
            adj_chip[:, 3:] - half * fx_inner[:, None],
            jnp.flip(adj_inner, 1),
        ],
        axis=1,
    )
    (grad_velocity,) = call(
        adjoint_kernel,
        [((3, 2, 8, 128), f32)],
        [pltpu.VMEM((3, 10, 24, 128), f32)] * 2 + wide_rows,
        (0,),
        (core_arg, adjoint, visc),
    )

    t_x = jnp.concatenate([tau_outer[:, None], tau_x, tau_other[:, None]], axis=1)
    t_y = jnp.concatenate([t_low, tau_y, t_high], axis=2)
    predicted = own_state - SCALE * (
        half * (t_x[:, 2:] - t_x[:, :2]) + 0.5 * (t_y[:, :, 2:] - t_y[:, :, :-2]) + along_z(tau_z)
    )
    results = call(
        finish_kernel,
        [
            ((9, 1, 128), f32),
            ((1, 128), f32),
            ((1, 128, 128), f32),
            ((1, 128), f32),
            ((6, 1, 128), f32),
            ((1, 128), f32),
        ],
        [],
        (),
        (whole,),
    )
    g_w_in, g_b_in, g_w_mid, g_b_mid, g_w_out, g_b_out = results
    return (
        mirror(predicted, 1),
        grad_velocity,
        jnp.transpose(g_w_in, (1, 0, 2)),
        g_b_in,
        g_w_mid,
        g_b_mid,
        jnp.transpose(g_w_out, (1, 2, 0)),
        g_b_out[:, :6],
    )


def solution(mesh):
    placed = (
        P(None, "gx", "yz", None),
        P("gx", "yz", None),
        P(None, "gx", "yz", None),
        P(("gx", "yz"), None),
        P("yz", None, None),
        P("yz", None),
        P("yz", None, None),
        P("yz", None),
        P("yz", None, None),
        P("yz", None),
    )
    return jax.shard_map(
        step,
        mesh=mesh,
        in_specs=placed,
        out_specs=(
            P(None, "gx", "yz", None),
            P(None, "gx", "yz", None),
            P("yz", None, None),
            P("yz", None),
            P("yz", None, None),
            P("yz", None),
            P("yz", None, None),
            P("yz", None),
        ),
        check_vma=False,
    )
```

```python
import jax
import jax.numpy as jnp
from jax import lax
from jax.experimental import pallas as pl
from jax.experimental.pallas import tpu as pltpu
from jax.sharding import PartitionSpec as P

SUBSTEPS = 4
STEP = 0.15
SCALE = 0.5
CAP = 2
PREC = lax.Precision.HIGH
AXES = ("gx", "yz")
INTERPRET = False
NEAR_WIDTH = (16, 14, 12, 10, 8)
NEAR_AT = (0, 64, 120, 168, 208)


def permute(value, target):
    n_gx, n_yz = lax.axis_size("gx"), lax.axis_size("yz")
    pairs = []
    for g in range(n_gx):
        for y in range(n_yz):
            to_g, to_y = target(g, y)
            pairs.append((g * n_yz + y, (to_g % n_gx) * n_yz + to_y % n_yz))
    return lax.ppermute(value, AXES, pairs)


def exchange(value, axis, groups=None):
    return lax.all_to_all(value, axis, 0, 0, axis_index_groups=groups, tiled=True)


def to_partner(value):
    return permute(value, lambda g, y: (g ^ 1, y))


def across(value):
    return permute(value, lambda g, y: (g - 1 if g % 2 == 0 else g + 1, y))


def packed(pieces):
    return jnp.concatenate([p.reshape(-1, 128) for p in pieces], axis=0)


def unpacked(buffer, shapes):
    pieces, at = [], 0
    for shape in shapes:
        rows = 1
        for n in shape[:-1]:
            rows *= n
        pieces.append(buffer[at : at + rows].reshape(shape))
        at += rows
    return pieces


def swap_y(low, high):
    below = permute(low, lambda g, y: (g, y + 1))
    above = permute(high, lambda g, y: (g, y - 1))
    return below, above


def spec(space):
    return pl.BlockSpec(memory_space=space)


def call(kernel, outs, scratch, smem_ins, args, smem_outs=(), vmem_outs=()):
    if not INTERPRET:
        args = [
            arg if i in smem_ins else pltpu.with_memory_space_constraint(arg, pltpu.VMEM)
            for i, arg in enumerate(args)
        ]
    vmem_outs = () if INTERPRET else vmem_outs
    return pl.pallas_call(
        kernel,
        out_shape=[
            (pltpu.VMEM if i in vmem_outs else jax.ShapeDtypeStruct)(shape, dtype)
            for i, (shape, dtype) in enumerate(outs)
        ],
        in_specs=[spec(pltpu.SMEM if i in smem_ins else pltpu.VMEM) for i in range(len(args))],
        out_specs=[spec(pltpu.SMEM if i in smem_outs else pltpu.VMEM) for i in range(len(outs))],
        scratch_shapes=scratch,
        interpret=INTERPRET,
    )(*args)


def turned(value, shift, axis):
    return pltpu.roll(value, shift % value.shape[axis], axis)


def coefficients(visc, rows, kx, ky, kz):
    for i in range(rows):
        own = visc[i]
        ky[i] = 0.5 * (own + turned(own, -1, 0))
        kz[i] = 0.5 * (own + turned(own, -1, 1))
        if i + 1 < rows:
            kx[i] = 0.5 * (own + visc[i + 1])


def diffusion(state, other, first, last, k_at, kx, ky, kz):
    for _ in range(SUBSTEPS):
        first, last = first + 1, last - 1
        for c in range(3):
            center = state[c, first]
            below = kx[k_at + first - 1] * (center - state[c, first - 1])
            for i in range(first, last + 1):
                k = k_at + i
                upper = state[c, i + 1]
                above = kx[k] * (upper - center)
                y_flux = ky[k] * (turned(center, -1, 0) - center)
                z_flux = kz[k] * (turned(center, -1, 1) - center)
                total = (above - below) + (y_flux - turned(y_flux, 1, 0))
                total = total + (z_flux - turned(z_flux, 1, 1))
                other[c, i] = center + STEP * total
                below, center = above, upper
        state, other = other, state
    return state


def placed(core, owner_ref, slot_ref, count):
    for e in range(count.shape[0]):
        count[e] = 0
    for k in range(16):
        owner = owner_ref[jnp.bitwise_xor(k, core * 8)]
        rank = count[owner]
        count[owner] = rank + 1
        slot_ref[k] = owner * CAP + rank


def stress_kernel(
    core_ref, owner_ref, cot, low, high, edge, mate, columns, slot_ref, c_wide, count
):
    core = core_ref[0]
    half = 0.5 * (1 - 2 * core).astype(jnp.float32)
    columns[96:112] = jnp.zeros((16, 128), jnp.float32)
    placed(core, owner_ref, slot_ref, count)
    for x in range(2):
        d = []
        for c in range(3):
            own = cot[c, x]
            c_wide[7:8] = low[40 + c * 2 + x : 41 + c * 2 + x]
            c_wide[8:16] = own
            c_wide[16:17] = high[40 + c * 2 + x : 41 + c * 2 + x]
            if x == 0:
                d_x = cot[c, 1] - edge[32 + c * 8 : 40 + c * 8]
            else:
                d_x = mate[176 + c * 8 : 184 + c * 8] - cot[c, 0]
            d_y = 0.5 * (c_wide[9:17] - c_wide[7:15])
            d_z = 0.5 * (turned(own, -1, 1) - turned(own, 1, 1))
            d.append((half * d_x, d_y, d_z))
        grads = (
            d[0][0], d[1][1], d[2][2],
            d[0][1] + d[1][0], d[0][2] + d[2][0], d[1][2] + d[2][1],
        )
        for k in range(6):
            columns[k * 16 + x * 8 : k * 16 + x * 8 + 8] = SCALE * grads[k]


def forward_kernel(
    core_ref, slot_ref, grad_columns, fields, low, high, mate, near, mate_in,
    send, own_state, visc,
    work, spare, kx, ky, kz, columns,
):
    half = 0.5 * (1 - 2 * core_ref[0]).astype(jnp.float32)
    send[...] = jnp.zeros_like(send)
    for f in range(4):
        row = (lambda i, f=f: visc.at[i]) if f == 3 else (lambda i, f=f: work.at[f, i])
        for j in range(5):
            at = NEAR_AT[j] + f * NEAR_WIDTH[j]
            row(4 - j)[4 + j : 20 - j] = near[at : at + NEAR_WIDTH[j]]
            if j < 3:
                row(9 + j)[4 + j : 20 - j] = mate_in[at : at + NEAR_WIDTH[j]]
        for x in range(2):
            at = f * 2 + x
            row(5 + x)[3:8] = low[at * 5 : at * 5 + 5]
            row(5 + x)[8:16] = fields[f, x]
            row(5 + x)[16:21] = high[at * 5 : at * 5 + 5]
            row(8 - x)[3:21] = mate[at * 18 : at * 18 + 18]
    coefficients(visc, 12, kx, ky, kz)
    state = diffusion(work, spare, 0, 11, 0, kx, ky, kz)

    for c in range(3):
        for x in range(2):
            at = (c * 3) * 16 + x * 8
            own = state[c, 5 + x, 8:16]
            own_state[c, x] = own
            columns[at : at + 8] = half * (state[c, 6 + x, 8:16] - state[c, 4 + x, 8:16])
            columns[at + 16 : at + 24] = 0.5 * (state[c, 5 + x, 9:17] - state[c, 5 + x, 7:15])
            columns[at + 32 : at + 40] = 0.5 * (turned(own, -1, 1) - turned(own, 1, 1))
    columns[144:256] = grad_columns[...]
    for k in range(16):
        send[slot_ref[k]] = columns[pl.ds(k, 16, stride=16)]


def adjoint_kernel(core_ref, adjoint, visc, out, work, spare, kx, ky, kz):
    for c in range(3):
        for i in range(10):
            work[c, i, 4:20] = adjoint[c, i]
    coefficients(visc, 12, kx, ky, kz)
    state = diffusion(work, spare, 0, 9, 1, kx, ky, kz)
    core = core_ref[0]
    for c in range(3):
        for x in range(2):
            out[c, jnp.bitwise_xor(x, core)] = state[c, 4 + x, 8:16]


def finish_kernel(whole, w_in, b_in, w_mid, b_mid, w_out, b_out):
    for i in range(9):
        w_in[i] = whole[i : i + 1]
    for i in range(6):
        w_out[i] = whole[139 + i : 140 + i]
    b_in[...] = whole[9:10]
    w_mid[0] = whole[10:138]
    b_mid[...] = whole[138:139]
    b_out[...] = whole[145:146]


def along_z(values):
    return 0.5 * (jnp.roll(values, -1, -1) - jnp.roll(values, 1, -1))


def step(velocity, viscosity, cotangent, assignment, w_in, b_in, w_mid, b_mid, w_out, b_out):
    experts = lax.axis_size("yz")
    core = lax.axis_index("gx") % 2
    sign = (1 - 2 * core).astype(jnp.float32)

    def mirror(v, dim):
        return jnp.where(core == 0, v, jnp.flip(v, dim))

    fields = jnp.concatenate([mirror(velocity, 1), mirror(viscosity, 0)[None]], axis=0)
    cot = mirror(cotangent, 1)
    core_arg = core.astype(jnp.int32).reshape(1)

    edge = across(packed([fields[:, 0], cot[:, 0]]))
    low, high = swap_y(
        packed([fields[:, :, 3:], cot[:, :, 7:]]), packed([fields[:, :, :5], cot[:, :, :1]])
    )
    f_low, f_high = low[:40].reshape(4, 2, 5, 128), high[:40].reshape(4, 2, 5, 128)
    wide = jnp.concatenate([f_low, fields, f_high], axis=2)
    mate = to_partner(packed([wide, edge[:32], cot[:, 1]]))
    partner = mate[:144].reshape(4, 2, 18, 128)
    chip = jnp.concatenate([wide, jnp.flip(partner, 1)], axis=1)
    reach = [chip[:, j, 1 + j : 17 - j] for j in range(4)]
    near = across(packed(reach + [mate[144:176]]))
    mate_in = to_partner(near[:168])
    f32, i32 = jnp.float32, jnp.int32
    grad_columns, slot = call(
        stress_kernel,
        [((112, 128), f32), ((16,), i32)],
        [pltpu.VMEM((24, 128), f32), pltpu.SMEM((experts,), i32)],
        (0, 1),
        (core_arg, assignment.reshape(16), cot, low, high, edge, mate),
        smem_outs=(1,),
        vmem_outs=(0,),
    )
    wide_rows = [pltpu.VMEM((12, 24, 128), f32)] * 3
    send, own_state, visc = call(
        forward_kernel,
        [((experts * CAP, 16, 128), f32), ((3, 2, 8, 128), f32), ((12, 24, 128), f32)],
        [pltpu.VMEM((3, 12, 24, 128), f32)] * 2 + wide_rows + [pltpu.VMEM((256, 128), f32)],
        (0, 1),
        (core_arg, slot, grad_columns, fields, low, high, mate, near, mate_in),
        vmem_outs=(1, 2),
    )
    recv = exchange(send.reshape(experts, CAP * 16, 128), "yz")
    turn = jnp.transpose(recv.reshape(experts * CAP, 16, 128), (1, 0, 2)).reshape(16, -1)
    x, sg = turn[:9], turn[9:15]

    w1, w2, w3 = w_in[0], w_mid[0], w_out[0]

    def dot(a, b, ca, cb):
        return lax.dot_general(a, b, (((ca,), (cb,)), ((), ())), precision=PREC)

    h1 = jnp.tanh(dot(w1, x, 0, 0) + b_in[0][:, None])
    h2 = jnp.tanh(dot(w2, h1, 0, 0) + b_mid[0][:, None])
    stress = dot(w3, h2, 0, 0) + b_out[0][:, None]
    g2 = dot(w3, sg, 1, 0) * (1.0 - h2 * h2)
    g1 = dot(w2, g2, 1, 0) * (1.0 - h1 * h1)
    fg = dot(w1, g1, 1, 0)
    grads = [
        dot(x, g1, 1, 1),
        jnp.sum(g1, axis=1)[None],
        dot(h1, g2, 1, 1),
        jnp.sum(g2, axis=1)[None],
        dot(sg, h2, 1, 1),
        jnp.pad(jnp.sum(sg, axis=1), (0, 122))[None],
    ]

    back = jnp.concatenate([fg, stress], axis=0).reshape(15, experts * CAP, 128)
    back = jnp.transpose(back, (1, 0, 2)).reshape(experts, CAP * 15, 128)
    home = exchange(back, "yz").reshape(experts * CAP, 15, 128)
    home = jnp.transpose(home[slot], (1, 0, 2)).reshape(15, 2, 8, 128)

    chips = lax.axis_size("gx") // 2
    vector = jnp.concatenate(grads, axis=0)
    chunk = -(-vector.shape[0] // chips)
    vector = vector + to_partner(vector)
    split = jnp.pad(vector, ((0, chunk * chips - vector.shape[0]), (0, 0))).reshape(chips, chunk, 128)
    groups = [list(range(0, 2 * chips, 2)), list(range(1, 2 * chips, 2))]
    parts = exchange(split, "gx", groups)
    mine = jnp.sum(parts, axis=0)
    whole = exchange(jnp.broadcast_to(mine, split.shape), "gx", groups).reshape(-1, 128)

    fgrad = home[:9].reshape(3, 3, 2, 8, 128)
    fx, fy, fz = fgrad[:, 0], fgrad[:, 1], fgrad[:, 2]
    tau = home[9:]
    tau_x = jnp.stack([tau[0], tau[3], tau[4]])
    tau_y = jnp.stack([tau[3], tau[1], tau[5]])
    tau_z = jnp.stack([tau[4], tau[5], tau[2]])
    part = cot - along_z(fz)
    low, high = swap_y(
        packed([part[:, :, 4:], fx[:, :, 4:], fy[:, :, 3:], tau_y[:, :, 7:]]),
        packed([part[:, :, :4], fx[:, :, :4], fy[:, :, :5], tau_y[:, :, :1]]),
    )
    rims = [(3, 2, 4, 128), (3, 2, 4, 128), (3, 2, 5, 128), (3, 2, 1, 128)]
    p_low, x_low, y_low, t_low = unpacked(low, rims)
    p_high, x_high, y_high, t_high = unpacked(high, rims)
    fy_wide = jnp.concatenate([y_low, fy, y_high], axis=2)
    part = jnp.concatenate([p_low, part, p_high], axis=2)
    part = part - 0.5 * (fy_wide[:, :, 2:] - fy_wide[:, :, :-2])
    fx_wide = jnp.concatenate([x_low, fx, x_high], axis=2)
    got = across(packed([fx[:, 0], tau_x[:, 0]]))
    fx_edge, tau_outer = unpacked(got, [(3, 8, 128), (3, 8, 128)])
    got = to_partner(packed([part, fx_wide, fx_edge, tau_x[:, 1]]))
    part_other, fx_other, fx_far, tau_other = unpacked(
        got, [part.shape, fx_wide.shape, (3, 8, 128), (3, 8, 128)]
    )
    part_chip = jnp.concatenate([part, jnp.flip(part_other, 1)], axis=1)
    fx_chip = jnp.concatenate([fx_wide, jnp.flip(fx_other, 1)], axis=1)
    half = 0.5 * sign
    zero = jnp.zeros_like(fx_chip[:, :1])
    fx_pad = jnp.concatenate([zero, fx_chip, zero], axis=1)
    adj_chip = part_chip - half * (fx_pad[:, 2:] - fx_pad[:, :-2])
    last = adj_chip[:, 3] - half * jnp.pad(fx_far, ((0, 0), (4, 4), (0, 0)))
    send = jnp.concatenate([adj_chip[:, :3], last[:, None]], axis=1)
    got = across(packed([send, fx_chip[:, 0]]))
    adj_outer, fx_outer = unpacked(got, [(3, 4, 16, 128), (3, 16, 128)])
    adj_outer = jnp.flip(adj_outer, 1)
    adj_outer = jnp.concatenate(
        [adj_outer[:, :3], adj_outer[:, 3:] - half * fx_chip[:, :1]], axis=1
    )
    got = to_partner(packed([adj_outer[:, 2:], fx_outer]))
    adj_inner, fx_inner = unpacked(got, [(3, 2, 16, 128), (3, 16, 128)])
    adjoint = jnp.concatenate(
        [
            adj_outer,
            adj_chip[:, :1] + half * fx_outer[:, None],
            adj_chip[:, 1:3],
            adj_chip[:, 3:] - half * fx_inner[:, None],
            jnp.flip(adj_inner, 1),
        ],
        axis=1,
    )
    (grad_velocity,) = call(
        adjoint_kernel,
        [((3, 2, 8, 128), f32)],
        [pltpu.VMEM((3, 10, 24, 128), f32)] * 2 + wide_rows,
        (0,),
        (core_arg, adjoint, visc),
    )

    t_x = jnp.concatenate([tau_outer[:, None], tau_x, tau_other[:, None]], axis=1)
    t_y = jnp.concatenate([t_low, tau_y, t_high], axis=2)
    predicted = own_state - SCALE * (
        half * (t_x[:, 2:] - t_x[:, :2]) + 0.5 * (t_y[:, :, 2:] - t_y[:, :, :-2]) + along_z(tau_z)
    )
    results = call(
        finish_kernel,
        [
            ((9, 1, 128), f32),
            ((1, 128), f32),
            ((1, 128, 128), f32),
            ((1, 128), f32),
            ((6, 1, 128), f32),
            ((1, 128), f32),
        ],
        [],
        (),
        (whole,),
    )
    g_w_in, g_b_in, g_w_mid, g_b_mid, g_w_out, g_b_out = results
    return (
        mirror(predicted, 1),
        grad_velocity,
        jnp.transpose(g_w_in, (1, 0, 2)),
        g_b_in,
        g_w_mid,
        g_b_mid,
        jnp.transpose(g_w_out, (1, 2, 0)),
        g_b_out[:, :6],
    )


def solution(mesh):
    placed = (
        P(None, "gx", "yz", None),
        P("gx", "yz", None),
        P(None, "gx", "yz", None),
        P(("gx", "yz"), None),
        P("yz", None, None),
        P("yz", None),
        P("yz", None, None),
        P("yz", None),
        P("yz", None, None),
        P("yz", None),
    )
    return jax.shard_map(
        step,
        mesh=mesh,
        in_specs=placed,
        out_specs=(
            P(None, "gx", "yz", None),
            P(None, "gx", "yz", None),
            P("yz", None, None),
            P("yz", None),
            P("yz", None, None),
            P("yz", None),
            P("yz", None, None),
            P("yz", None),
        ),
        check_vma=False,
    )
```
